512 devices in a mesh: gx: 16 (over z), gy: 32 (over y, x, core).
Axes of the slice: x: 4, y: 4, z: 16, core: 2. Of those that a mesh axis runs over, the one named last changes fastest.
Arguments:
- adjoint_guess: float32 [64, 512, 256], P('gx', 'gy'), may hold values from -80 to 80, as said below
- velocity: float32 [3, 64, 16384], P(None, 'gx', 'gy'), may hold values from -1 to 1
- leaf_rate: float32 [64, 16384], P('gx', 'gy'), may hold values from 0.2 to 5
- canopy: int32 [64, 16384], P('gx', 'gy'), may hold values from 0 to 1, as said below
- solid: int32 [64, 16384], P('gx', 'gy'), may hold values from 0 to 1, as said below
- receptors: int32 [8], replicated, may hold values from 0 to 32767
Outputs:
- adjoint_field: float32 [64, 512, 256], P('gx', 'gy')
- residual: float32 [64, 512, 256], P('gx', 'gy')
The draws below stay inside these ranges and needn't reach their ends.
Inputs may be any that keep to these rules, and one draw needn't show every extreme that they name: `adjoint_guess`: finite values. 1 marks building cells; every horizontal column is solid from the ground up to its building's height. `canopy`: 1 marks tree-crown cells; none is solid.
All inputs are finite; a program needn't handle non-finite values.
Results may differ from the reference program's by a relative error of at most 0.0003.
Values sent between devices are 32-bit elements; how exact they have to be, the bound alone decides.
A program may use at most 64 MiB of HBM per device.

```python
import math
import jax
import jax.numpy as jnp

NZ = 32
R = 8
CYCLES = 3
NX = 64
NY = 512


def street_columns(key):
    base_key = jax.random.fold_in(key, 11)
    keys = jax.random.split(base_key, 5)
    building = (jax.random.randint(keys[0], (NX, NY), 0, 4) == 0).astype(jnp.int32)
    height = jax.random.randint(keys[1], (NX, NY), 3, NZ // 2 + 1) * building
    tree = (jax.random.randint(keys[2], (NX, NY), 0, 3) == 0).astype(jnp.int32) * (1 - building)
    crown_top = jax.random.randint(keys[3], (NX, NY), 4, NZ // 2 + 1)
    crown_base = jax.random.randint(keys[4], (NX, NY), 1, 3)
    levels = jnp.arange(NZ, dtype=jnp.int32)
    solid_cells = (levels[None, None, :] < height[:, :, None]).astype(jnp.int32)
    crown = (levels[None, None, :] >= crown_base[:, :, None]) & (levels[None, None, :] < crown_top[:, :, None])
    canopy_cells = crown.astype(jnp.int32) * tree[:, :, None]
    return (solid_cells.reshape(NX, NY * NZ), canopy_cells.reshape(NX, NY * NZ))


def draw_solid(key, part):
    return street_columns(key)[0]


def draw_canopy(key, part):
    return street_columns(key)[1]


def draw_adjoint_guess(key, part):
    row_pos = jnp.arange(NX, dtype=jnp.float32) / max(NX - 1, 1)
    col_pos = jnp.arange(NY, dtype=jnp.float32) / max(NY - 1, 1)
    lane_pos = (jnp.arange(NZ * R) % R).astype(jnp.float32) / R
    base = jnp.clip(jax.random.normal(key, (NX, NY, NZ * R), jnp.float32), -4.0, 4.0)
    scale = jnp.exp(jnp.log(3.0) * row_pos)[:, None, None] * jnp.exp(jnp.log(3.0) * col_pos)[None, :, None]
    return (base * scale * (1.0 + lane_pos)[None, None, :]).astype(jnp.float32)


def place_ends(entries, rng, least, largest):
    longest = entries.shape.index(max(entries.shape))
    spots = []
    for shift in (0, 1):
        where = [jax.random.randint(jax.random.fold_in(rng, axis), (), 0, length) for axis, length in enumerate(entries.shape)]
        where[longest] = (where[longest] + shift) % entries.shape[longest]
        spots.append(tuple(where))
    return entries.at[spots[0]].set(least).at[spots[1]].set(largest)


def block_levels(rng, shape, cuts, least, largest):
    factor_of, own = 1.0, jax.random.fold_in(rng, 6)
    for position, blocks in cuts:
        draws = jnp.exp(jax.random.uniform(jax.random.fold_in(own, position), (blocks,), jnp.float32, least / len(cuts), largest / len(cuts)))
        factor_of = factor_of * jnp.repeat(draws, shape[position] // blocks).reshape([-1 if axis == position else 1 for axis in range(len(shape))])
    return factor_of


def setup_inputs(seed: int = 0) -> dict:
    streams_of = jax.random.split(jax.random.key(seed), 7)
    adjoint_guess = draw_adjoint_guess(jax.random.fold_in(streams_of[6], 71), 0)
    velocity = jnp.clip(jax.random.uniform(streams_of[1], (3, NX, NY * NZ), jnp.float32, -1.0, 1.0) * block_levels(streams_of[1], (3, NX, NY * NZ), ((1, 16), (2, 32)), -0.4, 0.0), -1.0, 1.0)
    leaf_rate = jnp.clip(jnp.exp(math.log(5.0) - 3.218876 * jax.random.uniform(streams_of[2], (NX, NY * NZ), jnp.float32) ** block_levels(streams_of[2], (NX, NY * NZ), ((0, 16), (1, 32)), -0.2, 0.2)), 0.2, 5.0)
    canopy = draw_canopy(jax.random.fold_in(streams_of[6], 71), 0)
    solid = draw_solid(jax.random.fold_in(streams_of[6], 71), 0)
    receptors = place_ends(jax.random.randint(streams_of[5], (R,), 0, NX * NY), jax.random.fold_in(streams_of[5], 1), 0, (NX * NY) - 1).astype(jnp.int32)
    return {"adjoint_guess": adjoint_guess, "velocity": velocity, "leaf_rate": leaf_rate, "canopy": canopy, "solid": solid, "receptors": receptors}


horiz_diff = 4.0
vert_diff = 2.0
decay_rate = 3.5
penalty = 40.0
leaf_gain = 4.0
source_gain = 32.0


def coefficient_fields(flows, reaction):
    east_flow = flows[0]
    north_flow = flows[1]
    rise_flow = flows[2]
    couplings = [horiz_diff + jax.nn.relu(east_flow), horiz_diff + jax.nn.relu(-east_flow),
                 horiz_diff + jax.nn.relu(north_flow), horiz_diff + jax.nn.relu(-north_flow),
                 vert_diff + jax.nn.relu(rise_flow), vert_diff + jax.nn.relu(-rise_flow)]
    diagonal = decay_rate + reaction + couplings[0] + couplings[1] + couplings[2] + couplings[3] + couplings[4] + couplings[5]
    return [jnp.repeat(piece, R, axis=-1) for piece in [diagonal] + couplings]


def apply_operator(padded, coefficients):
    centre = padded[1:-1, 1:-1]
    zero_lane = jnp.zeros(centre.shape[:-1] + (R,), jnp.float32)
    upper_cells = jnp.concatenate([centre[..., R:], zero_lane], axis=-1)
    lower_cells = jnp.concatenate([zero_lane, centre[..., :-R]], axis=-1)
    diagonal, east_c, west_c, north_c, south_c, upper_c, lower_c = coefficients
    return (diagonal * centre - east_c * padded[2:, 1:-1] - west_c * padded[:-2, 1:-1]
            - north_c * padded[1:-1, 2:] - south_c * padded[1:-1, :-2]
            - upper_c * upper_cells - lower_c * lower_cells)


def per_receptor(first, second):
    return jnp.sum((first * second).reshape(-1, R), axis=0)


def spread_lanes(values):
    return jnp.tile(values, NZ)


def reference(adjoint_guess, velocity, leaf_rate, canopy, solid, receptors):
    flows = velocity.reshape(3, NX, NY, NZ)
    reaction = (penalty * solid.astype(jnp.float32) + leaf_gain * leaf_rate * canopy.astype(jnp.float32)).reshape(NX, NY, NZ)
    coefficients = coefficient_fields(flows, reaction)

    def operate(values):
        return apply_operator(jnp.pad(values, ((1, 1), (1, 1), (0, 0))), coefficients)

    rec_rows = (receptors // NY).astype(jnp.int32)
    rec_cols = (receptors % NY).astype(jnp.int32)
    lanes = (R + jnp.arange(R)).astype(jnp.int32)
    source = jnp.zeros((NX, NY, NZ * R), jnp.float32).at[rec_rows, rec_cols, lanes].add(source_gain)
    iterate = adjoint_guess
    residual = source - operate(iterate)
    for cycle_index in range(CYCLES):
        image_dir = operate(residual)
        alpha_step = per_receptor(residual, residual) / per_receptor(residual, image_dir)
        halfway = residual - spread_lanes(alpha_step) * image_dir
        turned = operate(halfway)
        omega_step = per_receptor(turned, halfway) / per_receptor(turned, turned)
        iterate = iterate + spread_lanes(alpha_step) * residual + spread_lanes(omega_step) * halfway
        residual = halfway - spread_lanes(omega_step) * turned
    return iterate, residual
```

```python
import functools

import jax
import jax.numpy as jnp
from jax import lax
from jax.experimental import pallas as pl
from jax.experimental.pallas import tpu as pltpu
from jax.sharding import PartitionSpec as P

NZ = 32
R = 8
CYCLES = 3
DEGREE = 2 * CYCLES

horiz_diff = 4.0
vert_diff = 2.0
decay_rate = 3.5
penalty = 40.0
leaf_gain = 4.0
source_gain = 32.0

SHIFT = 46.5
SCALE = 32.0

PAD_R = 4
PAD_C = 8
LANES = 128

PAIRS = [(a, b) for a in range(DEGREE + 1) for b in range(a + 1)]
SLOT = {pair: n for n, pair in enumerate(PAIRS)}
SIDES = [(dx, dy) for dx in (1, -1, 0) for dy in (0, 1, -1) if (dx, dy) != (0, 0)]


def window(delta, reach, own, pad):
    if delta == 0:
        return pl.ds(pad, own), pl.ds(pad, own)
    if delta > 0:
        return pl.ds(pad + own - reach, reach), pl.ds(pad - reach, reach)
    return pl.ds(pad, reach), pl.ds(pad + own, reach)


def kernel(
    nx, ny, rows, cols,
    guess, velocity, leaf, canopy, solid, receptors,
    field_out, residual_out,
    start, basis, packed, coef, raw_vel, raw_leaf, raw_canopy, raw_solid,
    gram, mine, plane_in, line, line_in,
    load_sem, halo_send, halo_recv, plane_send, plane_recv, line_send, line_recv,
):
    gx = lax.axis_index("gx")
    gy = lax.axis_index("gy")

    def peer(dx, dy):
        return {
            "gx": lax.rem(gx + dx + nx, nx) if dx else gx,
            "gy": lax.rem(gy + dy + ny, ny) if dy else gy,
        }

    barrier = pltpu.get_barrier_semaphore()
    greeted = [(0, d) for d in range(1, ny)] + [(d, 0) for d in range(1, nx)]
    greeted += [side for side in SIDES if side[0] and side[1]]
    for side in greeted:
        pl.semaphore_signal(barrier, inc=1, device_id=peer(*side), device_id_type=pl.DeviceIdType.MESH)

    own_r, own_c = pl.ds(PAD_R, rows), pl.ds(PAD_C, cols)
    loads = [
        pltpu.make_async_copy(velocity, raw_vel, load_sem.at[0]),
        pltpu.make_async_copy(leaf, raw_leaf, load_sem.at[1]),
        pltpu.make_async_copy(canopy, raw_canopy, load_sem.at[2]),
        pltpu.make_async_copy(solid, raw_solid, load_sem.at[3]),
        pltpu.make_async_copy(guess, start.at[own_r, own_c], load_sem.at[4]),
    ]
    for copy in loads:
        copy.start()

    sub = lax.broadcasted_iota(jnp.int32, (8, LANES), 0)
    lane = lax.broadcasted_iota(jnp.int32, (8, LANES), 1)

    for copy in loads[:4]:
        copy.wait()
    reaction = penalty * raw_solid[...].astype(jnp.float32) + leaf_gain * raw_leaf[...] * raw_canopy[...].astype(jnp.float32)
    parts = [raw_vel[0], raw_vel[1], raw_vel[2], reaction]
    spread = (sub % 4) * NZ + lane % NZ
    for i in range(rows):
        for tile in range(cols // 8):
            total = None
            for n, part in enumerate(parts):
                low = jnp.broadcast_to(part[i : i + 1, (2 * tile) * LANES : (2 * tile + 1) * LANES], (8, LANES))
                high = jnp.broadcast_to(part[i : i + 1, (2 * tile + 1) * LANES : (2 * tile + 2) * LANES], (8, LANES))
                value = jnp.take_along_axis(jnp.where(sub < 4, low, high), spread, axis=1)
                total = value if total is None else jnp.where(lane // NZ == n, value, total)
            packed[PAD_R + i, PAD_C + 8 * tile : PAD_C + 8 * tile + 8, :] = total

    loads[4].wait()
    pl.semaphore_wait(barrier, len(greeted))

    def exchange(ref, bank, reach):
        copies = []
        for n, (dx, dy) in enumerate(SIDES):
            near = reach - 1 if dx and dy else reach
            src_r, dst_r = window(dx, near, rows, PAD_R)
            src_c, dst_c = window(dy, near, cols, PAD_C)
            copies.append(
                pltpu.make_async_remote_copy(
                    src_ref=ref.at[src_r, src_c],
                    dst_ref=ref.at[dst_r, dst_c],
                    send_sem=halo_send.at[bank, n],
                    recv_sem=halo_recv.at[bank, n],
                    device_id=peer(dx, dy),
                    device_id_type=pl.DeviceIdType.MESH,
                )
            )
        for copy in copies:
            copy.start()
        return copies

    moving = exchange(packed, 0, 3) + exchange(start, 1, 4)
    for copy in moving:
        copy.wait_recv()

    inv = 1.0 / SCALE
    first_row = jnp.where(gx == 0, 0.0, inv)
    last_row = jnp.where(gx == nx - 1, 0.0, inv)
    first_col = jnp.where(gy == 0, 0.0, inv)
    last_col = jnp.where(gy == ny - 1, 0.0, inv)
    tiles = (cols + 2 * PAD_C) // 8
    first_tile, last_tile = PAD_C // 8, (PAD_C + cols) // 8 - 1
    for r in range(PAD_R - 3, PAD_R + rows + 3):
        outer = r in (PAD_R - 3, PAD_R + rows + 2)
        for tile in range(first_tile, last_tile + 1) if outer else range(tiles):
            here = pl.ds(8 * tile, 8)
            cell = packed[r, 8 * tile : 8 * tile + 8, :]
            for half in range(2):
                span = slice(half * LANES, (half + 1) * LANES)
                level = lane // R + half * (LANES // R)
                u, v, w, react = (jnp.take_along_axis(cell, n * NZ + level, axis=1) for n in range(4))
                relu = lambda value: jnp.maximum(value, 0.0)
                east, west = horiz_diff + relu(u), horiz_diff + relu(-u)
                north, south = horiz_diff + relu(v), horiz_diff + relu(-v)
                up, down = vert_diff + relu(w), vert_diff + relu(-w)
                diag = decay_rate + react + east + west + north + south + up + down
                coef[0, r, here, span] = (diag - SHIFT) * inv
                coef[1, r, here, span] = east * (last_row if r == PAD_R + rows - 1 else inv)
                coef[2, r, here, span] = west * (first_row if r == PAD_R else inv)
                coef[3, r, here, span] = north * (jnp.where(sub == 7, last_col, inv) if tile == last_tile else inv)
                coef[4, r, here, span] = south * (jnp.where(sub == 0, first_col, inv) if tile == first_tile else inv)
                coef[5, r, here, span] = up * (jnp.where(lane >= LANES - R, 0.0, inv) if half else inv)
                coef[6, r, here, span] = down * (inv if half else jnp.where(lane < R, 0.0, inv))

    def apply(ref, r, inner):
        height = cols + 2 * PAD_C
        width = NZ * R
        cut = slice(PAD_C, PAD_C + cols) if inner else slice(0, height)
        centre = ref[r]
        north = pltpu.roll(centre, height - 1, 0)[cut]
        south = pltpu.roll(centre, 1, 0)[cut]
        middle = centre[cut]
        up = pltpu.roll(middle, width - R, 1)
        down = pltpu.roll(middle, R, 1)
        return (
            coef[0, r, cut, :] * middle
            - coef[1, r, cut, :] * ref[r + 1, cut, :]
            - coef[2, r, cut, :] * ref[r - 1, cut, :]
            - coef[3, r, cut, :] * north
            - coef[4, r, cut, :] * south
            - coef[5, r, cut, :] * up
            - coef[6, r, cut, :] * down
        )

    height = cols + 2 * PAD_C
    lanes = lax.broadcasted_iota(jnp.int32, (height, NZ * R), 1)
    place = lax.broadcasted_iota(jnp.int32, (height, NZ * R), 0) + (gy * cols - PAD_C)
    aim = jnp.full((height, NZ * R), -1 << 30, jnp.int32)
    for q in range(R):
        aim = jnp.where(lanes == R + q, receptors[q], aim)
    aim = aim - place
    for r in range(PAD_R - 3, PAD_R + rows + 3):
        source = jnp.where(aim == (gx * rows + (r - PAD_R)) * (ny * cols), source_gain, 0.0)
        basis[0, r] = source - (SCALE * apply(start, r, False) + SHIFT * start[r])

    def advance(j, reach):
        for r in range(PAD_R - reach, PAD_R + rows + reach):
            if reach:
                basis[j, r] = apply(basis.at[j - 1], r, False)
            else:
                basis[j, r, PAD_C : PAD_C + cols, :] = apply(basis.at[j - 1], r, True)

    def products(pairs):
        sums = {}
        for r in range(PAD_R, PAD_R + rows):
            for c in range(PAD_C, PAD_C + cols, 8):
                for half in range(2):
                    span = slice(half * LANES, (half + 1) * LANES)
                    held = {}
                    for a, b in pairs:
                        for j in (a, b):
                            if j not in held:
                                held[j] = basis[j, r, c : c + 8, span]
                        term = held[a] * held[b]
                        sums[a, b] = term if (a, b) not in sums else sums[a, b] + term
        for pair in pairs:
            n = SLOT[pair]
            gram[n : n + 1, :] = jnp.sum(sums[pair], axis=0, keepdims=True)

    advance(1, 2)
    advance(2, 1)
    advance(3, 0)
    moving_2 = exchange(basis.at[3], 2, 3)
    gram[...] = jnp.zeros_like(gram)
    early = [pair for pair in PAIRS if pair[0] <= 3]
    products(early)
    for copy in moving_2:
        copy.wait_recv()
    advance(4, 2)
    advance(5, 1)
    advance(6, 0)
    products([pair for pair in PAIRS if pair[0] > 3])

    def fold(value):
        for step in (64, 32, 16, 8):
            value = value + pltpu.roll(value, step, 1)
        return value

    entry = lax.broadcasted_iota(jnp.int32, (32, LANES), 0)
    group = lax.broadcasted_iota(jnp.int32, (32, LANES), 1) // R
    chosen = group == entry % 16
    local = jnp.where(chosen, fold(gram[...]), 0.0)
    mine[0:1, :] = jnp.sum(local[0:16], axis=0, keepdims=True)
    mine[1:2, :] = jnp.sum(local[16:32], axis=0, keepdims=True)

    def gather(src, dst, index, count, send_sem, recv_sem, to):
        copies = [
            pltpu.make_async_remote_copy(
                src_ref=src,
                dst_ref=dst.at[index],
                send_sem=send_sem,
                recv_sem=recv_sem,
                device_id=to(d),
                device_id_type=pl.DeviceIdType.MESH,
            )
            for d in sorted(range(1, count), key=lambda d: -min(d, count - d))
        ]
        for copy in copies:
            copy.start()
        dst[index] = src[...]
        some = dst.at[pl.ds(0, count - 1)]
        pltpu.make_async_copy(some, some, recv_sem).wait()
        parts = [dst[n] for n in range(count)]
        while len(parts) > 1:
            parts = [parts[n] + parts[n + 1] for n in range(0, len(parts), 2)]
        return parts[0], pltpu.make_async_copy(some, some, send_sem)

    plane_sum, plane_left = gather(mine, plane_in, gy, ny, plane_send, plane_recv, lambda d: peer(0, d))
    line[...] = plane_sum
    total, line_left = gather(line, line_in, gx, nx, line_send, line_recv, lambda d: peer(d, 0))

    wide = jnp.concatenate(
        [jnp.broadcast_to(total[0:1], (16, LANES)), jnp.broadcast_to(total[1:2], (16, LANES))], axis=0
    )
    gram[...] = fold(jnp.where(chosen, wide, 0.0))
    g = lambda a, b: gram[SLOT[max(a, b), min(a, b)] : SLOT[max(a, b), min(a, b)] + 1, :]

    shift = SHIFT / SCALE

    def operate(d):
        out = []
        for j in range(len(d) + 1):
            terms = ([shift * d[j]] if j < len(d) else []) + ([d[j - 1]] if j else [])
            out.append(terms[0] if len(terms) == 1 else terms[0] + terms[1])
        return out

    def add(terms):
        while len(terms) > 1:
            terms = [terms[n] + terms[n + 1] if n + 1 < len(terms) else terms[n] for n in range(0, len(terms), 2)]
        return terms[0]

    d = [jnp.ones((1, LANES), jnp.float32)]
    y = [jnp.zeros((1, LANES), jnp.float32) for _ in range(DEGREE)]
    for _ in range(CYCLES):
        image = operate(d)
        pulled = [add([g(i, j) * d[j] for j in range(len(d))]) for i in range(len(image))]
        squares = add([d[i] * pulled[i] for i in range(len(d))])
        against = add([image[i] * pulled[i] for i in range(len(image))])
        alpha = squares / against
        half_way = [(d[i] if i < len(d) else 0.0) - alpha * image[i] for i in range(len(image))]
        turned = operate(half_way)
        pulled = [add([g(i, j) * turned[j] for j in range(len(turned))]) for i in range(len(turned))]
        along = add([half_way[i] * pulled[i] for i in range(len(half_way))])
        power = add([turned[i] * pulled[i] for i in range(len(turned))])
        omega = along / power
        for i in range(len(d)):
            y[i] = y[i] + alpha * d[i]
        for i in range(len(half_way)):
            y[i] = y[i] + omega * half_way[i]
        d = [(half_way[i] if i < len(half_way) else 0.0) - omega * turned[i] for i in range(len(turned))]

    steps = [value * inv for value in y]
    for r in range(rows):
        for c in range(0, cols, 8):
            for half in range(2):
                span = slice(half * LANES, (half + 1) * LANES)
                held = [basis[j, PAD_R + r, PAD_C + c : PAD_C + c + 8, span] for j in range(DEGREE + 1)]
                moved = add([steps[j] * held[j] for j in range(DEGREE)])
                field_out[r, c : c + 8, span] = start[PAD_R + r, PAD_C + c : PAD_C + c + 8, span] + moved
                residual_out[r, c : c + 8, span] = add([d[j] * held[j] for j in range(DEGREE + 1)])

    for copy in moving + moving_2:
        copy.wait_send()
    plane_left.wait()
    line_left.wait()


def solution(mesh):
    nx, ny = mesh.shape["gx"], mesh.shape["gy"]

    def body(adjoint_guess, velocity, leaf_rate, canopy, solid, receptors):
        rows, cols = adjoint_guess.shape[0], adjoint_guess.shape[1]
        tall, wide = rows + 2 * PAD_R, cols + 2 * PAD_C
        shape = jax.ShapeDtypeStruct(adjoint_guess.shape, jnp.float32)
        return pl.pallas_call(
            functools.partial(kernel, nx, ny, rows, cols),
            out_shape=(shape, shape),
            in_specs=[pl.BlockSpec(memory_space=pl.ANY)] * 5 + [pl.BlockSpec(memory_space=pltpu.SMEM)],
            out_specs=[pl.BlockSpec(memory_space=pltpu.VMEM)] * 2,
            scratch_shapes=[
                pltpu.VMEM((tall, wide, NZ * R), jnp.float32),
                pltpu.VMEM((DEGREE + 1, tall, wide, NZ * R), jnp.float32),
                pltpu.VMEM((tall, wide, LANES), jnp.float32),
                pltpu.VMEM((7, tall, wide, NZ * R), jnp.float32),
                pltpu.VMEM(velocity.shape, jnp.float32),
                pltpu.VMEM(leaf_rate.shape, jnp.float32),
                pltpu.VMEM(canopy.shape, jnp.int32),
                pltpu.VMEM(solid.shape, jnp.int32),
                pltpu.VMEM((32, LANES), jnp.float32),
                pltpu.VMEM((2, LANES), jnp.float32),
                pltpu.VMEM((ny, 2, LANES), jnp.float32),
                pltpu.VMEM((2, LANES), jnp.float32),
                pltpu.VMEM((nx, 2, LANES), jnp.float32),
                pltpu.SemaphoreType.DMA((5,)),
                pltpu.SemaphoreType.DMA((3, len(SIDES))),
                pltpu.SemaphoreType.DMA((3, len(SIDES))),
                pltpu.SemaphoreType.DMA,
                pltpu.SemaphoreType.DMA,
                pltpu.SemaphoreType.DMA,
                pltpu.SemaphoreType.DMA,
            ],
            compiler_params=pltpu.CompilerParams(collective_id=0, has_side_effects=True),
        )(adjoint_guess, velocity, leaf_rate, canopy, solid, receptors)

    return jax.shard_map(
        body,
        mesh=mesh,
        in_specs=(
            P("gx", "gy", None),
            P(None, "gx", "gy"),
            P("gx", "gy"),
            P("gx", "gy"),
            P("gx", "gy"),
            P(),
        ),
        out_specs=(P("gx", "gy", None), P("gx", "gy", None)),
        check_vma=False,
    )
```

```python
import functools

import jax
import jax.numpy as jnp
from jax import lax
from jax.experimental import pallas as pl
from jax.experimental.pallas import tpu as pltpu
from jax.sharding import PartitionSpec as P

NZ = 32
R = 8
CYCLES = 3
DEGREE = 2 * CYCLES

horiz_diff = 4.0
vert_diff = 2.0
decay_rate = 3.5
penalty = 40.0
leaf_gain = 4.0
source_gain = 32.0

SHIFT = 27.0
SCALE = 16.0

PAD_R = 4
PAD_C = 8
LANES = 128

PAIRS = [(a, b) for a in range(DEGREE + 1) for b in range(a + 1)]
SLOT = {pair: n for n, pair in enumerate(PAIRS)}
SIDES = [(dx, dy) for dx in (1, -1, 0) for dy in (0, 1, -1) if (dx, dy) != (0, 0)]


def window(delta, reach, own, pad):
    if delta == 0:
        return pl.ds(pad, own), pl.ds(pad, own)
    if delta > 0:
        return pl.ds(pad + own - reach, reach), pl.ds(pad - reach, reach)
    return pl.ds(pad, reach), pl.ds(pad + own, reach)


def two_sum(a, b):
    total = a + b
    back = total - a
    return total, (a - (total - back)) + (b - back)


def pair_add(a, b):
    total, error = two_sum(a[0], b[0])
    return total, error + (a[1] + b[1])


def split(value):
    scaled = value * 4097.0
    high = scaled - (scaled - value)
    return high, value - high


def tree(terms, join):
    terms = list(terms)
    while len(terms) > 1:
        terms = [join(terms[n], terms[n + 1]) if n + 1 < len(terms) else terms[n] for n in range(0, len(terms), 2)]
    return terms[0]


def kernel(
    nx, ny, rows, cols,
    guess, velocity, leaf, canopy, solid, receptors,
    field_out, residual_out,
    start, basis, packed, coef, raw_vel, raw_leaf, raw_canopy, raw_solid,
    halves, gram, mine, plane_in, line, line_in,
    load_sem, halo_send, halo_recv, plane_send, plane_recv, line_send, line_recv, met_x, met_y,
):
    gx = lax.axis_index("gx")
    gy = lax.axis_index("gy")

    def peer(dx, dy):
        return {
            "gx": lax.rem(gx + dx + nx, nx) if dx else gx,
            "gy": lax.rem(gy + dy + ny, ny) if dy else gy,
        }

    barrier = pltpu.get_barrier_semaphore()
    for side in SIDES:
        pl.semaphore_signal(barrier, inc=1, device_id=peer(*side), device_id_type=pl.DeviceIdType.MESH)

    def rounds(count):
        reach, out = 1, []
        while reach < count // 2:
            out.append(reach)
            reach *= 2
        return out

    def tell(n):
        for sem, far, to in ((met_x, rounds(nx), lambda d: (d, 0)), (met_y, rounds(ny), lambda d: (0, d))):
            if n < len(far):
                for d in (far[n], -far[n]):
                    pl.semaphore_signal(sem.at[n], inc=1, device_id=peer(*to(d)), device_id_type=pl.DeviceIdType.MESH)

    def hear(n):
        for sem, far in ((met_x, rounds(nx)), (met_y, rounds(ny))):
            if n < len(far):
                pl.semaphore_wait(sem.at[n], 2)

    rest = max(len(rounds(nx)), len(rounds(ny)))

    own_r, own_c = pl.ds(PAD_R, rows), pl.ds(PAD_C, cols)
    loads = [
        pltpu.make_async_copy(velocity, raw_vel, load_sem.at[0]),
        pltpu.make_async_copy(leaf, raw_leaf, load_sem.at[1]),
        pltpu.make_async_copy(canopy, raw_canopy, load_sem.at[2]),
        pltpu.make_async_copy(solid, raw_solid, load_sem.at[3]),
        pltpu.make_async_copy(guess, start.at[own_r, own_c], load_sem.at[4]),
    ]
    for copy in loads:
        copy.start()

    sub = lax.broadcasted_iota(jnp.int32, (8, LANES), 0)
    lane = lax.broadcasted_iota(jnp.int32, (8, LANES), 1)

    for copy in loads[:4]:
        copy.wait()
    reaction = penalty * raw_solid[...].astype(jnp.float32) + leaf_gain * raw_leaf[...] * raw_canopy[...].astype(jnp.float32)
    parts = [raw_vel[0], raw_vel[1], raw_vel[2], reaction]
    spread = (sub % 4) * NZ + lane % NZ
    for i in range(rows):
        for tile in range(cols // 8):
            total = None
            for n, part in enumerate(parts):
                low = jnp.broadcast_to(part[i : i + 1, (2 * tile) * LANES : (2 * tile + 1) * LANES], (8, LANES))
                high = jnp.broadcast_to(part[i : i + 1, (2 * tile + 1) * LANES : (2 * tile + 2) * LANES], (8, LANES))
                value = jnp.take_along_axis(jnp.where(sub < 4, low, high), spread, axis=1)
                total = value if total is None else jnp.where(lane // NZ == n, value, total)
            packed[PAD_R + i, PAD_C + 8 * tile : PAD_C + 8 * tile + 8, :] = total

    loads[4].wait()
    pl.semaphore_wait(barrier, len(SIDES))

    def exchange(ref, bank, reach):
        copies = []
        for n, (dx, dy) in enumerate(SIDES):
            near = reach - 1 if dx and dy else reach
            src_r, dst_r = window(dx, near, rows, PAD_R)
            src_c, dst_c = window(dy, near, cols, PAD_C)
            copies.append(
                pltpu.make_async_remote_copy(
                    src_ref=ref.at[src_r, src_c],
                    dst_ref=ref.at[dst_r, dst_c],
                    send_sem=halo_send.at[bank, n],
                    recv_sem=halo_recv.at[bank, n],
                    device_id=peer(dx, dy),
                    device_id_type=pl.DeviceIdType.MESH,
                )
            )
        for copy in copies:
            copy.start()
        return copies

    moving_0 = exchange(packed, 0, 3)
    moving_1 = exchange(start, 1, 4)
    tell(0)

    inv = 1.0 / SCALE
    first_row = jnp.where(gx == 0, 0.0, inv)
    last_row = jnp.where(gx == nx - 1, 0.0, inv)
    first_col = jnp.where(gy == 0, 0.0, inv)
    last_col = jnp.where(gy == ny - 1, 0.0, inv)
    tiles = (cols + 2 * PAD_C) // 8
    first_tile, last_tile = PAD_C // 8, (PAD_C + cols) // 8 - 1
    own_cells = [(r, tile) for r in range(PAD_R, PAD_R + rows) for tile in range(first_tile, last_tile + 1)]
    all_cells = [
        (r, tile)
        for r in range(PAD_R - 3, PAD_R + rows + 3)
        for tile in range(tiles)
        if PAD_R - 3 < r < PAD_R + rows + 2 or first_tile <= tile <= last_tile
    ]

    def expand(cells):
        for r, tile in cells:
            here = pl.ds(8 * tile, 8)
            cell = packed[r, 8 * tile : 8 * tile + 8, :]
            for half in range(2):
                span = slice(half * LANES, (half + 1) * LANES)
                level = lane // R + half * (LANES // R)
                u, v, w, react = (jnp.take_along_axis(cell, n * NZ + level, axis=1) for n in range(4))
                relu = lambda value: jnp.maximum(value, 0.0)
                east, west = horiz_diff + relu(u), horiz_diff + relu(-u)
                north, south = horiz_diff + relu(v), horiz_diff + relu(-v)
                up, down = vert_diff + relu(w), vert_diff + relu(-w)
                diag = decay_rate + react + east + west + north + south + up + down
                coef[0, r, here, span] = (diag - SHIFT) * inv
                coef[1, r, here, span] = east * (last_row if r == PAD_R + rows - 1 else inv)
                coef[2, r, here, span] = west * (first_row if r == PAD_R else inv)
                coef[3, r, here, span] = north * (jnp.where(sub == 7, last_col, inv) if tile == last_tile else inv)
                coef[4, r, here, span] = south * (jnp.where(sub == 0, first_col, inv) if tile == first_tile else inv)
                coef[5, r, here, span] = up * (jnp.where(lane >= LANES - R, 0.0, inv) if half else inv)
                coef[6, r, here, span] = down * (inv if half else jnp.where(lane < R, 0.0, inv))

    expand(own_cells)
    hear(0)
    tell(1)
    for copy in moving_0:
        copy.wait_recv()
    expand([cell for cell in all_cells if cell not in own_cells])
    for copy in moving_1:
        copy.wait_recv()
    hear(1)
    tell(2)

    def apply(ref, r, inner):
        height = cols + 2 * PAD_C
        width = NZ * R
        cut = slice(PAD_C, PAD_C + cols) if inner else slice(0, height)
        centre = ref[r]
        north = pltpu.roll(centre, height - 1, 0)[cut]
        south = pltpu.roll(centre, 1, 0)[cut]
        middle = centre[cut]
        up = pltpu.roll(middle, width - R, 1)
        down = pltpu.roll(middle, R, 1)
        return (
            coef[0, r, cut, :] * middle
            - coef[1, r, cut, :] * ref[r + 1, cut, :]
            - coef[2, r, cut, :] * ref[r - 1, cut, :]
            - coef[3, r, cut, :] * north
            - coef[4, r, cut, :] * south
            - coef[5, r, cut, :] * up
            - coef[6, r, cut, :] * down
        )

    height = cols + 2 * PAD_C
    lanes = lax.broadcasted_iota(jnp.int32, (height, NZ * R), 1)
    place = lax.broadcasted_iota(jnp.int32, (height, NZ * R), 0) + (gy * cols - PAD_C)
    aim = jnp.full((height, NZ * R), -1 << 30, jnp.int32)
    for q in range(R):
        aim = jnp.where(lanes == R + q, receptors[q], aim)
    aim = aim - place
    for r in range(PAD_R - 3, PAD_R + rows + 3):
        source = jnp.where(aim == (gx * rows + (r - PAD_R)) * (ny * cols), source_gain, 0.0)
        basis[0, r] = source - (SCALE * apply(start, r, False) + SHIFT * start[r])

    def advance(j, reach):
        for r in range(PAD_R - reach, PAD_R + rows + reach):
            if reach:
                basis[j, r] = apply(basis.at[j - 1], r, False)
            else:
                basis[j, r, PAD_C : PAD_C + cols, :] = apply(basis.at[j - 1], r, True)

    def products(a):
        spots = [
            (r, c, half)
            for r in range(PAD_R, PAD_R + rows)
            for c in range(PAD_C, PAD_C + cols, 8)
            for half in range(2)
        ]
        for b in range(a + 1):
            sums[a, b] = None
        for n, (r, c, half) in enumerate(spots):
            high, low = split(basis[a, r, c : c + 8, half * LANES : (half + 1) * LANES])
            halves[a, n, 0], halves[a, n, 1] = high, low
            for b in range(a + 1):
                if b == a:
                    exact, cross, rest = high * high, 2.0 * (high * low), low * low
                else:
                    high_b, low_b = halves[b, n, 0], halves[b, n, 1]
                    exact, cross, rest = high * high_b, high * low_b + low * high_b, low * low_b
                if sums[a, b] is None:
                    sums[a, b] = (exact, cross + rest)
                else:
                    total, error = two_sum(sums[a, b][0], exact)
                    sums[a, b] = (total, sums[a, b][1] + (error + (cross + rest)))

    def turn(value, shift, axis):
        return pltpu.roll(value, shift % value.shape[axis], axis)

    def weave(x, y, bit, axis):
        low = ((sub if axis == 0 else lane) & bit) == 0
        near = tuple(jnp.where(low, u, v) for u, v in zip(x, y))
        far = tuple(jnp.where(low, turn(u, -bit, axis), turn(v, bit, axis)) for u, v in zip(x, y))
        return pair_add(near, far)

    def stack(pairs):
        zero = jnp.zeros((8, LANES), jnp.float32)
        got = [sums[pair] if pair else (zero, zero) for pair in pairs]
        for bit in (4, 2, 1):
            got = [weave(got[n], got[n + bit], bit, 0) for n in range(bit)]
        return got[0]

    sums = {}
    blocks = [PAIRS[n : n + 8] for n in range(0, len(PAIRS), 8)]
    blocks[-1] += [None] * (8 - len(blocks[-1]))
    advance(1, 2)
    advance(2, 1)
    advance(3, 0)
    moving_2 = exchange(basis.at[3], 2, 3)
    for a in range(4):
        products(a)
    stacked = [stack(blocks[0])]
    for copy in moving_2:
        copy.wait_recv()
    hear(2)
    tell(3)
    advance(4, 2)
    products(4)
    advance(5, 1)
    products(5)
    advance(6, 0)
    products(6)
    stacked += [stack(block) for block in blocks[1:]]

    quarter = [weave(stacked[n], stacked[n + 2], 64, 1) for n in range(2)]
    folded = weave(quarter[0], quarter[1], 32, 1)
    folded = weave(folded, folded, 16, 1)
    folded = weave(folded, folded, 8, 1)
    chosen = (lane // R) % 4 == sub % 4
    for n, value in enumerate(folded):
        value = jnp.where(chosen, value, 0.0)
        mine[n, 0:1, :] = jnp.sum(value[0:4], axis=0, keepdims=True)
        mine[n, 1:2, :] = jnp.sum(value[4:8], axis=0, keepdims=True)

    def gather(src, dst, index, count, send_sem, recv_sem, to):
        copies = [
            pltpu.make_async_remote_copy(
                src_ref=src,
                dst_ref=dst.at[index],
                send_sem=send_sem,
                recv_sem=recv_sem,
                device_id=to(d),
                device_id_type=pl.DeviceIdType.MESH,
            )
            for d in sorted(range(1, count), key=lambda d: -min(d, count - d))
        ]
        for copy in copies:
            copy.start()
        dst[index] = src[...]
        some = dst.at[pl.ds(0, count - 1)]
        pltpu.make_async_copy(some, some, recv_sem).wait()
        total = tree([(dst[n, 0], dst[n, 1]) for n in range(count)], pair_add)
        return total, pltpu.make_async_copy(some, some, send_sem)

    line_sum, line_left = gather(mine, line_in, gx, nx, line_send, line_recv, lambda d: peer(d, 0))
    line[0], line[1] = line_sum
    for n in range(3, rest):
        hear(n)
        tell(n + 1)
    total, plane_left = gather(line, plane_in, gy, ny, plane_send, plane_recv, lambda d: peer(0, d))

    value, error = total
    value, error = two_sum(value, error)
    upper = sub < 4
    for z in range(4):
        index = 32 * z + R * (sub % 4) + lane % R
        spread_out = lambda x: jnp.take_along_axis(
            jnp.where(upper, jnp.broadcast_to(x[0:1], (8, LANES)), jnp.broadcast_to(x[1:2], (8, LANES))), index, axis=1
        )
        here = spread_out(value)
        gram[0, 8 * z : 8 * z + 8, :] = here
        gram[1, 8 * z : 8 * z + 8, :] = spread_out(error)
        gram[2, 8 * z : 8 * z + 8, :], gram[3, 8 * z : 8 * z + 8, :] = split(here)

    def product(a, b):
        whole, high, low = b
        top = a[0] * whole
        return top, (((a[2] * high - top) + a[2] * low + a[3] * high) + a[3] * low) + a[1] * whole

    def entry(i, j):
        n = SLOT[max(i, j), min(i, j)]
        return tuple(gram[k, n : n + 1, :] for k in range(4))

    def with_halves(values):
        return [(value,) + split(value) for value in values]

    def pull(values, count):
        out = []
        for i in range(count):
            total, error = tree([product(entry(i, j), value) for j, value in enumerate(values)], pair_add)
            total, error = two_sum(total, error)
            out.append((total, error) + split(total))
        return out

    def inner(pulled, values):
        total, error = tree([product(a, b) for a, b in zip(pulled, values)], pair_add)
        return total + error

    shift = SHIFT / SCALE

    def operate(d):
        out = []
        for j in range(len(d) + 1):
            terms = ([shift * d[j]] if j < len(d) else []) + ([d[j - 1]] if j else [])
            out.append(terms[0] if len(terms) == 1 else terms[0] + terms[1])
        return out

    d = [jnp.ones((1, LANES), jnp.float32)]
    y = [jnp.zeros((1, LANES), jnp.float32) for _ in range(DEGREE)]
    for _ in range(CYCLES):
        image = operate(d)
        held, moved = with_halves(d), with_halves(image)
        pulled = pull(held, len(image))
        alpha = inner(pulled, held) / inner(pulled, moved)
        half_way = [(d[i] - alpha * image[i]) if i < len(d) else -(alpha * image[i]) for i in range(len(image))]
        turned = operate(half_way)
        held, moved = with_halves(half_way), with_halves(turned)
        pulled = pull(moved, len(turned))
        omega = inner(pulled, held) / inner(pulled, moved)
        for i in range(len(d)):
            y[i] = y[i] + alpha * d[i]
        for i in range(len(half_way)):
            y[i] = y[i] + omega * half_way[i]
        d = [
            (half_way[i] - omega * turned[i]) if i < len(half_way) else -(omega * turned[i])
            for i in range(len(turned))
        ]

    steps = [value * inv for value in y]
    for r in range(rows):
        for c in range(0, cols, 8):
            for half in range(2):
                span = slice(half * LANES, (half + 1) * LANES)
                held = [basis[j, PAD_R + r, PAD_C + c : PAD_C + c + 8, span] for j in range(DEGREE + 1)]
                moved = tree([steps[j] * held[j] for j in range(DEGREE)], jnp.add)
                field_out[r, c : c + 8, span] = start[PAD_R + r, PAD_C + c : PAD_C + c + 8, span] + moved
                residual_out[r, c : c + 8, span] = tree([d[j] * held[j] for j in range(DEGREE + 1)], jnp.add)

    for copy in moving_0 + moving_1 + moving_2:
        copy.wait_send()
    plane_left.wait()
    line_left.wait()


def solution(mesh):
    nx, ny = mesh.shape["gx"], mesh.shape["gy"]

    def body(adjoint_guess, velocity, leaf_rate, canopy, solid, receptors):
        rows, cols = adjoint_guess.shape[0], adjoint_guess.shape[1]
        tall, wide = rows + 2 * PAD_R, cols + 2 * PAD_C
        shape = jax.ShapeDtypeStruct(adjoint_guess.shape, jnp.float32)
        return pl.pallas_call(
            functools.partial(kernel, nx, ny, rows, cols),
            out_shape=(shape, shape),
            in_specs=[pl.BlockSpec(memory_space=pl.ANY)] * 5 + [pl.BlockSpec(memory_space=pltpu.SMEM)],
            out_specs=[pl.BlockSpec(memory_space=pltpu.VMEM)] * 2,
            scratch_shapes=[
                pltpu.VMEM((tall, wide, NZ * R), jnp.float32),
                pltpu.VMEM((DEGREE + 1, tall, wide, NZ * R), jnp.float32),
                pltpu.VMEM((tall, wide, LANES), jnp.float32),
                pltpu.VMEM((7, tall, wide, NZ * R), jnp.float32),
                pltpu.VMEM(velocity.shape, jnp.float32),
                pltpu.VMEM(leaf_rate.shape, jnp.float32),
                pltpu.VMEM(canopy.shape, jnp.int32),
                pltpu.VMEM(solid.shape, jnp.int32),
                pltpu.VMEM((DEGREE + 1, rows * cols * 2 // 8, 2, 8, LANES), jnp.float32),
                pltpu.VMEM((4, 32, LANES), jnp.float32),
                pltpu.VMEM((2, 2, LANES), jnp.float32),
                pltpu.VMEM((ny, 2, 2, LANES), jnp.float32),
                pltpu.VMEM((2, 2, LANES), jnp.float32),
                pltpu.VMEM((nx, 2, 2, LANES), jnp.float32),
                pltpu.SemaphoreType.DMA((5,)),
                pltpu.SemaphoreType.DMA((3, len(SIDES))),
                pltpu.SemaphoreType.DMA((3, len(SIDES))),
                pltpu.SemaphoreType.DMA,
                pltpu.SemaphoreType.DMA,
                pltpu.SemaphoreType.DMA,
                pltpu.SemaphoreType.DMA,
                pltpu.SemaphoreType.REGULAR((8,)),
                pltpu.SemaphoreType.REGULAR((8,)),
            ],
            compiler_params=pltpu.CompilerParams(collective_id=0, has_side_effects=True),
        )(adjoint_guess, velocity, leaf_rate, canopy, solid, receptors)

    return jax.shard_map(
        body,
        mesh=mesh,
        in_specs=(
            P("gx", "gy", None),
            P(None, "gx", "gy"),
            P("gx", "gy"),
            P("gx", "gy"),
            P("gx", "gy"),
            P(),
        ),
        out_specs=(P("gx", "gy", None), P("gx", "gy", None)),
        check_vma=False,
    )
```

```python
import functools

import jax
import jax.numpy as jnp
from jax import lax
from jax.experimental import pallas as pl
from jax.experimental.pallas import tpu as pltpu
from jax.sharding import PartitionSpec as P

NZ = 32
R = 8
CYCLES = 3
DEGREE = 2 * CYCLES

horiz_diff = 4.0
vert_diff = 2.0
decay_rate = 3.5
penalty = 40.0
leaf_gain = 4.0
source_gain = 32.0

SHIFT = 27.0
SCALE = 16.0

PAD_R = 4
PAD_C = 8
LANES = 128

PAIRS = [(a, b) for a in range(DEGREE + 1) for b in range(a + 1)]
SLOT = {pair: n for n, pair in enumerate(PAIRS)}
SIDES = [(1, 1), (1, -1), (-1, 1), (-1, -1), (0, 1), (0, -1), (1, 0), (-1, 0)]


def window(delta, reach, own, pad):
    if delta == 0:
        return pl.ds(pad, own), pl.ds(pad, own)
    if delta > 0:
        return pl.ds(pad + own - reach, reach), pl.ds(pad - reach, reach)
    return pl.ds(pad, reach), pl.ds(pad + own, reach)


def two_sum(a, b):
    total = a + b
    back = total - a
    return total, (a - (total - back)) + (b - back)


def pair_add(a, b):
    total, error = two_sum(a[0], b[0])
    return total, error + (a[1] + b[1])


def split(value):
    scaled = value * 4097.0
    high = scaled - (scaled - value)
    return high, value - high


def tree(terms, join):
    terms = list(terms)
    while len(terms) > 1:
        terms = [join(terms[n], terms[n + 1]) if n + 1 < len(terms) else terms[n] for n in range(0, len(terms), 2)]
    return terms[0]


def kernel(
    nx, ny, rows, cols,
    guess, velocity, leaf, canopy, solid, receptors,
    field_out, residual_out,
    start, basis, packed, coef, raw_vel, raw_leaf, raw_canopy, raw_solid,
    halves, gram, mine, plane_in, line, line_in, aims,
    load_sem, halo_send, halo_recv, plane_send, plane_recv, line_send, line_recv, met_x, met_y,
):
    gx = lax.axis_index("gx")
    gy = lax.axis_index("gy")

    def peer(dx, dy):
        return {
            "gx": lax.rem(gx + dx + nx, nx) if dx else gx,
            "gy": lax.rem(gy + dy + ny, ny) if dy else gy,
        }

    def inside(dy):
        return jnp.logical_and(gy + dy >= 0, gy + dy < ny)

    def where_inside(dy, act):
        if dy:
            pl.when(inside(dy))(act)
        else:
            act()

    def signal(sem, side):
        where_inside(
            side[1],
            lambda: pl.semaphore_signal(sem, inc=1, device_id=peer(*side), device_id_type=pl.DeviceIdType.MESH),
        )

    def both(d):
        return inside(d).astype(jnp.int32) + inside(-d).astype(jnp.int32)

    barrier = pltpu.get_barrier_semaphore()
    for side in SIDES:
        signal(barrier, side)

    def rounds(most):
        reach, out = 1, []
        while reach < most:
            out.append(reach)
            reach *= 2
        return out

    rounds_x, rounds_y = rounds(nx // 2), rounds(ny - 1)

    def tell(n):
        if n < len(rounds_x):
            for d in (rounds_x[n], -rounds_x[n]):
                signal(met_x.at[n], (d, 0))
        if n < len(rounds_y):
            for d in (rounds_y[n], -rounds_y[n]):
                signal(met_y.at[n], (0, d))

    def hear(n):
        if n < len(rounds_x):
            pl.semaphore_wait(met_x.at[n], 2)
        if n < len(rounds_y):
            pl.semaphore_wait(met_y.at[n], both(rounds_y[n]))

    rest = max(len(rounds_x), len(rounds_y))

    own_r, own_c = pl.ds(PAD_R, rows), pl.ds(PAD_C, cols)
    loads = [
        pltpu.make_async_copy(velocity, raw_vel, load_sem.at[0]),
        pltpu.make_async_copy(leaf, raw_leaf, load_sem.at[1]),
        pltpu.make_async_copy(canopy, raw_canopy, load_sem.at[2]),
        pltpu.make_async_copy(solid, raw_solid, load_sem.at[3]),
        pltpu.make_async_copy(guess, start.at[own_r, own_c], load_sem.at[4]),
        pltpu.make_async_copy(receptors, aims, load_sem.at[5]),
    ]
    for copy in loads:
        copy.start()

    def clear(side):
        for ref in (start, packed, basis.at[3]):
            ref[:, side, :] = jnp.zeros((ref.shape[0], PAD_C, ref.shape[2]), jnp.float32)

    pl.when(gy == 0)(lambda: clear(slice(0, PAD_C)))
    pl.when(gy == ny - 1)(lambda: clear(slice(PAD_C + cols, 2 * PAD_C + cols)))

    sub = lax.broadcasted_iota(jnp.int32, (8, LANES), 0)
    lane = lax.broadcasted_iota(jnp.int32, (8, LANES), 1)

    for copy in loads[:4]:
        copy.wait()
    reaction = penalty * raw_solid[...].astype(jnp.float32) + leaf_gain * raw_leaf[...] * raw_canopy[...].astype(jnp.float32)
    parts = [raw_vel[0], raw_vel[1], raw_vel[2], reaction]
    spread = (sub % 4) * NZ + lane % NZ
    for i in range(rows):
        for tile in range(cols // 8):
            total = None
            for n, part in enumerate(parts):
                low = jnp.broadcast_to(part[i : i + 1, (2 * tile) * LANES : (2 * tile + 1) * LANES], (8, LANES))
                high = jnp.broadcast_to(part[i : i + 1, (2 * tile + 1) * LANES : (2 * tile + 2) * LANES], (8, LANES))
                value = jnp.take_along_axis(jnp.where(sub < 4, low, high), spread, axis=1)
                total = value if total is None else jnp.where(lane // NZ == n, value, total)
            packed[PAD_R + i, PAD_C + 8 * tile : PAD_C + 8 * tile + 8, :] = total

    for copy in loads[4:]:
        copy.wait()
    pl.semaphore_wait(barrier, 3 * (1 + both(1)) - 1)

    def exchange(ref, bank, reach):
        copies = []
        for n, (dx, dy) in enumerate(SIDES):
            near = reach - 1 if dx and dy else reach
            src_r, dst_r = window(dx, near, rows, PAD_R)
            src_c, dst_c = window(dy, near, cols, PAD_C)
            copies.append(
                (
                    dy,
                    pltpu.make_async_remote_copy(
                        src_ref=ref.at[src_r, src_c],
                        dst_ref=ref.at[dst_r, dst_c],
                        send_sem=halo_send.at[bank, n],
                        recv_sem=halo_recv.at[bank, n],
                        device_id=peer(dx, dy),
                        device_id_type=pl.DeviceIdType.MESH,
                    ),
                )
            )
        for dy, copy in copies:
            where_inside(dy, copy.start)
        return copies

    def arrive(copies):
        for dy, copy in copies:
            where_inside(-dy, copy.wait_recv)

    moving_0 = exchange(packed, 0, 3)
    moving_1 = exchange(start, 1, 4)
    tell(0)

    inv = 1.0 / SCALE
    first_row = jnp.where(gx == 0, 0.0, inv)
    last_row = jnp.where(gx == nx - 1, 0.0, inv)
    first_col = jnp.where(gy == 0, 0.0, inv)
    last_col = jnp.where(gy == ny - 1, 0.0, inv)
    tiles = (cols + 2 * PAD_C) // 8
    first_tile, last_tile = PAD_C // 8, (PAD_C + cols) // 8 - 1
    own_cells = [(r, tile) for r in range(PAD_R, PAD_R + rows) for tile in range(first_tile, last_tile + 1)]
    all_cells = [
        (r, tile)
        for r in range(PAD_R - 3, PAD_R + rows + 3)
        for tile in range(tiles)
        if PAD_R - 3 < r < PAD_R + rows + 2 or first_tile <= tile <= last_tile
    ]

    def expand(cells):
        for r, tile in cells:
            here = pl.ds(8 * tile, 8)
            cell = packed[r, 8 * tile : 8 * tile + 8, :]
            for half in range(2):
                span = slice(half * LANES, (half + 1) * LANES)
                level = lane // R + half * (LANES // R)
                u, v, w, react = (jnp.take_along_axis(cell, n * NZ + level, axis=1) for n in range(4))
                relu = lambda value: jnp.maximum(value, 0.0)
                east, west = horiz_diff + relu(u), horiz_diff + relu(-u)
                north, south = horiz_diff + relu(v), horiz_diff + relu(-v)
                up, down = vert_diff + relu(w), vert_diff + relu(-w)
                diag = decay_rate + react + east + west + north + south + up + down
                coef[0, r, here, span] = (diag - SHIFT) * inv
                coef[1, r, here, span] = east * (last_row if r == PAD_R + rows - 1 else inv)
                coef[2, r, here, span] = west * (first_row if r == PAD_R else inv)
                coef[3, r, here, span] = north * (jnp.where(sub == 7, last_col, inv) if tile == last_tile else inv)
                coef[4, r, here, span] = south * (jnp.where(sub == 0, first_col, inv) if tile == first_tile else inv)
                coef[5, r, here, span] = up * (jnp.where(lane >= LANES - R, 0.0, inv) if half else inv)
                coef[6, r, here, span] = down * (inv if half else jnp.where(lane < R, 0.0, inv))

    expand(own_cells)
    hear(0)
    tell(1)
    arrive(moving_0)
    expand([cell for cell in all_cells if cell not in own_cells])
    arrive(moving_1)
    hear(1)
    tell(2)

    def apply(ref, r, inner):
        height = cols + 2 * PAD_C
        width = NZ * R
        cut = slice(PAD_C, PAD_C + cols) if inner else slice(0, height)
        centre = ref[r]
        north = pltpu.roll(centre, height - 1, 0)[cut]
        south = pltpu.roll(centre, 1, 0)[cut]
        middle = centre[cut]
        up = pltpu.roll(middle, width - R, 1)
        down = pltpu.roll(middle, R, 1)
        return (
            coef[0, r, cut, :] * middle
            - coef[1, r, cut, :] * ref[r + 1, cut, :]
            - coef[2, r, cut, :] * ref[r - 1, cut, :]
            - coef[3, r, cut, :] * north
            - coef[4, r, cut, :] * south
            - coef[5, r, cut, :] * up
            - coef[6, r, cut, :] * down
        )

    height = cols + 2 * PAD_C
    lanes = lax.broadcasted_iota(jnp.int32, (height, NZ * R), 1)
    place = lax.broadcasted_iota(jnp.int32, (height, NZ * R), 0) + (gy * cols - PAD_C)
    aim = jnp.full((height, NZ * R), -1 << 30, jnp.int32)
    for q in range(R):
        aim = jnp.where(lanes == R + q, aims[q], aim)
    aim = aim - place
    for r in range(PAD_R - 3, PAD_R + rows + 3):
        source = jnp.where(aim == (gx * rows + (r - PAD_R)) * (ny * cols), source_gain, 0.0)
        basis[0, r] = source - (SCALE * apply(start, r, False) + SHIFT * start[r])

    def advance(j, reach):
        for r in range(PAD_R - reach, PAD_R + rows + reach):
            if reach:
                basis[j, r] = apply(basis.at[j - 1], r, False)
            else:
                basis[j, r, PAD_C : PAD_C + cols, :] = apply(basis.at[j - 1], r, True)

    def products(a):
        spots = [
            (r, c, half)
            for r in range(PAD_R, PAD_R + rows)
            for c in range(PAD_C, PAD_C + cols, 8)
            for half in range(2)
        ]
        for b in range(a + 1):
            sums[a, b] = None
        for n, (r, c, half) in enumerate(spots):
            high, low = split(basis[a, r, c : c + 8, half * LANES : (half + 1) * LANES])
            halves[a, n, 0], halves[a, n, 1] = high, low
            for b in range(a + 1):
                if b == a:
                    exact, cross, rest = high * high, 2.0 * (high * low), low * low
                else:
                    high_b, low_b = halves[b, n, 0], halves[b, n, 1]
                    exact, cross, rest = high * high_b, high * low_b + low * high_b, low * low_b
                if sums[a, b] is None:
                    sums[a, b] = (exact, cross + rest)
                else:
                    total, error = two_sum(sums[a, b][0], exact)
                    sums[a, b] = (total, sums[a, b][1] + (error + (cross + rest)))

    def turn(value, shift, axis):
        return pltpu.roll(value, shift % value.shape[axis], axis)

    def weave(x, y, bit, axis):
        low = ((sub if axis == 0 else lane) & bit) == 0
        near = tuple(jnp.where(low, u, v) for u, v in zip(x, y))
        far = tuple(jnp.where(low, turn(u, -bit, axis), turn(v, bit, axis)) for u, v in zip(x, y))
        return pair_add(near, far)

    def stack(pairs):
        zero = jnp.zeros((8, LANES), jnp.float32)
        got = [sums[pair] if pair else (zero, zero) for pair in pairs]
        for bit in (4, 2, 1):
            got = [weave(got[n], got[n + bit], bit, 0) for n in range(bit)]
        return got[0]

    sums = {}
    blocks = [PAIRS[n : n + 8] for n in range(0, len(PAIRS), 8)]
    blocks[-1] += [None] * (8 - len(blocks[-1]))
    advance(1, 2)
    advance(2, 1)
    advance(3, 0)
    moving_2 = exchange(basis.at[3], 2, 3)
    for a in range(4):
        products(a)
    stacked = [stack(blocks[0])]
    arrive(moving_2)
    hear(2)
    tell(3)
    advance(4, 2)
    products(4)
    advance(5, 1)
    products(5)
    advance(6, 0)
    products(6)
    hear(3)
    tell(4)
    stacked += [stack(block) for block in blocks[1:]]

    quarter = [weave(stacked[n], stacked[n + 2], 64, 1) for n in range(2)]
    folded = weave(quarter[0], quarter[1], 32, 1)
    folded = weave(folded, folded, 16, 1)
    folded = weave(folded, folded, 8, 1)
    chosen = (lane // R) % 4 == sub % 4
    for n, value in enumerate(folded):
        value = jnp.where(chosen, value, 0.0)
        mine[n, 0:1, :] = jnp.sum(value[0:4], axis=0, keepdims=True)
        mine[n, 1:2, :] = jnp.sum(value[4:8], axis=0, keepdims=True)

    def gather(src, dst, index, count, send_sem, recv_sem, to):
        copies = [
            pltpu.make_async_remote_copy(
                src_ref=src,
                dst_ref=dst.at[index],
                send_sem=send_sem,
                recv_sem=recv_sem,
                device_id=to(d),
                device_id_type=pl.DeviceIdType.MESH,
            )
            for d in sorted(range(1, count), key=lambda d: -min(d, count - d))
        ]
        for copy in copies:
            copy.start()
        dst[index] = src[...]
        some = dst.at[pl.ds(0, count - 1)]
        pltpu.make_async_copy(some, some, recv_sem).wait()
        total = tree([(dst[n, 0], dst[n, 1]) for n in range(count)], pair_add)
        return total, pltpu.make_async_copy(some, some, send_sem)

    line_sum, line_left = gather(mine, line_in, gx, nx, line_send, line_recv, lambda d: peer(d, 0))
    line[0], line[1] = line_sum
    for n in range(4, rest):
        hear(n)
        tell(n + 1)
    total, plane_left = gather(line, plane_in, gy, ny, plane_send, plane_recv, lambda d: peer(0, d))

    value, error = total
    value, error = two_sum(value, error)
    upper = sub < 4
    for z in range(4):
        index = 32 * z + R * (sub % 4) + lane % R
        spread_out = lambda x: jnp.take_along_axis(
            jnp.where(upper, jnp.broadcast_to(x[0:1], (8, LANES)), jnp.broadcast_to(x[1:2], (8, LANES))), index, axis=1
        )
        here = spread_out(value)
        gram[0, 8 * z : 8 * z + 8, :] = here
        gram[1, 8 * z : 8 * z + 8, :] = spread_out(error)
        gram[2, 8 * z : 8 * z + 8, :], gram[3, 8 * z : 8 * z + 8, :] = split(here)

    def product(a, b):
        whole, high, low = b
        top = a[0] * whole
        return top, (((a[2] * high - top) + a[2] * low + a[3] * high) + a[3] * low) + a[1] * whole

    def entry(i, j):
        n = SLOT[max(i, j), min(i, j)]
        return tuple(gram[k, n : n + 1, :] for k in range(4))

    def with_halves(values):
        return [(value,) + split(value) for value in values]

    def pull(values, count):
        out = []
        for i in range(count):
            total, error = tree([product(entry(i, j), value) for j, value in enumerate(values)], pair_add)
            total, error = two_sum(total, error)
            out.append((total, error) + split(total))
        return out

    def inner(pulled, values):
        total, error = tree([product(a, b) for a, b in zip(pulled, values)], pair_add)
        return total + error

    shift = SHIFT / SCALE

    def operate(d):
        out = []
        for j in range(len(d) + 1):
            terms = ([shift * d[j]] if j < len(d) else []) + ([d[j - 1]] if j else [])
            out.append(terms[0] if len(terms) == 1 else terms[0] + terms[1])
        return out

    d = [jnp.ones((1, LANES), jnp.float32)]
    y = [jnp.zeros((1, LANES), jnp.float32) for _ in range(DEGREE)]
    for _ in range(CYCLES):
        image = operate(d)
        held, moved = with_halves(d), with_halves(image)
        pulled = pull(held, len(image))
        alpha = inner(pulled, held) / inner(pulled, moved)
        half_way = [(d[i] - alpha * image[i]) if i < len(d) else -(alpha * image[i]) for i in range(len(image))]
        turned = operate(half_way)
        held, moved = with_halves(half_way), with_halves(turned)
        pulled = pull(moved, len(turned))
        omega = inner(pulled, held) / inner(pulled, moved)
        for i in range(len(d)):
            y[i] = y[i] + alpha * d[i]
        for i in range(len(half_way)):
            y[i] = y[i] + omega * half_way[i]
        d = [
            (half_way[i] - omega * turned[i]) if i < len(half_way) else -(omega * turned[i])
            for i in range(len(turned))
        ]

    steps = [value * inv for value in y]
    for r in range(rows):
        for c in range(0, cols, 8):
            for half in range(2):
                span = slice(half * LANES, (half + 1) * LANES)
                held = [basis[j, PAD_R + r, PAD_C + c : PAD_C + c + 8, span] for j in range(DEGREE + 1)]
                moved = tree([steps[j] * held[j] for j in range(DEGREE)], jnp.add)
                field_out[r, c : c + 8, span] = start[PAD_R + r, PAD_C + c : PAD_C + c + 8, span] + moved
                residual_out[r, c : c + 8, span] = tree([d[j] * held[j] for j in range(DEGREE + 1)], jnp.add)

    for dy, copy in moving_0 + moving_1 + moving_2:
        where_inside(dy, copy.wait_send)
    plane_left.wait()
    line_left.wait()


def solution(mesh):
    nx, ny = mesh.shape["gx"], mesh.shape["gy"]

    def body(*arrays):
        adjoint_guess, velocity, leaf_rate, canopy, solid, receptors = arrays
        rows, cols = adjoint_guess.shape[0], adjoint_guess.shape[1]
        tall, wide = rows + 2 * PAD_R, cols + 2 * PAD_C
        shape = jax.ShapeDtypeStruct(adjoint_guess.shape, jnp.float32)
        return pl.pallas_call(
            functools.partial(kernel, nx, ny, rows, cols),
            out_shape=(shape, shape),
            in_specs=[pl.BlockSpec(memory_space=pltpu.HBM)] * 6,
            out_specs=[pl.BlockSpec(memory_space=pltpu.VMEM)] * 2,
            scratch_shapes=[
                pltpu.VMEM((tall, wide, NZ * R), jnp.float32),
                pltpu.VMEM((DEGREE + 1, tall, wide, NZ * R), jnp.float32),
                pltpu.VMEM((tall, wide, LANES), jnp.float32),
                pltpu.VMEM((7, tall, wide, NZ * R), jnp.float32),
                pltpu.VMEM(velocity.shape, jnp.float32),
                pltpu.VMEM(leaf_rate.shape, jnp.float32),
                pltpu.VMEM(canopy.shape, jnp.int32),
                pltpu.VMEM(solid.shape, jnp.int32),
                pltpu.VMEM((DEGREE + 1, rows * cols * 2 // 8, 2, 8, LANES), jnp.float32),
                pltpu.VMEM((4, 32, LANES), jnp.float32),
                pltpu.VMEM((2, 2, LANES), jnp.float32),
                pltpu.VMEM((ny, 2, 2, LANES), jnp.float32),
                pltpu.VMEM((2, 2, LANES), jnp.float32),
                pltpu.VMEM((nx, 2, 2, LANES), jnp.float32),
                pltpu.SMEM(receptors.shape, jnp.int32),
                pltpu.SemaphoreType.DMA((6,)),
                pltpu.SemaphoreType.DMA((3, len(SIDES))),
                pltpu.SemaphoreType.DMA((3, len(SIDES))),
                pltpu.SemaphoreType.DMA,
                pltpu.SemaphoreType.DMA,
                pltpu.SemaphoreType.DMA,
                pltpu.SemaphoreType.DMA,
                pltpu.SemaphoreType.REGULAR((8,)),
                pltpu.SemaphoreType.REGULAR((8,)),
            ],
            compiler_params=pltpu.CompilerParams(collective_id=0, has_side_effects=True, vmem_limit_bytes=16 << 20),
        )(*(pltpu.with_memory_space_constraint(array, pltpu.HBM) for array in arrays))

    return jax.shard_map(
        body,
        mesh=mesh,
        in_specs=(
            P("gx", "gy", None),
            P(None, "gx", "gy"),
            P("gx", "gy"),
            P("gx", "gy"),
            P("gx", "gy"),
            P(),
        ),
        out_specs=(P("gx", "gy", None), P("gx", "gy", None)),
        check_vma=False,
    )
```

```python
import functools

import jax
import jax.numpy as jnp
from jax import lax
from jax.experimental import pallas as pl
from jax.experimental.pallas import tpu as pltpu
from jax.sharding import PartitionSpec as P

NZ = 32
R = 8
CYCLES = 3
DEGREE = 2 * CYCLES

horiz_diff = 4.0
vert_diff = 2.0
decay_rate = 3.5
penalty = 40.0
leaf_gain = 4.0
source_gain = 32.0

SHIFT = 27.0
SCALE = 16.0

FIRST = 4
PAD_R = 4
PAD_C = 8
LANES = 128

PAIRS = [(a, b) for a in range(DEGREE + 1) for b in range(a + 1)]
SLOT = {pair: n for n, pair in enumerate(PAIRS)}
SIDES = [(1, 1), (1, -1), (-1, 1), (-1, -1), (0, 1), (0, -1), (1, 0), (-1, 0)]


def window(delta, reach, own, pad):
    if delta == 0:
        return pl.ds(pad, own), pl.ds(pad, own)
    if delta > 0:
        return pl.ds(pad + own - reach, reach), pl.ds(pad - reach, reach)
    return pl.ds(pad, reach), pl.ds(pad + own, reach)


def two_sum(a, b):
    total = a + b
    back = total - a
    return total, (a - (total - back)) + (b - back)


def pair_add(a, b):
    total, error = two_sum(a[0], b[0])
    return total, error + (a[1] + b[1])


def split(value):
    scaled = value * 4097.0
    high = scaled - (scaled - value)
    return high, value - high


def tree(terms, join):
    terms = list(terms)
    while len(terms) > 1:
        terms = [join(terms[n], terms[n + 1]) if n + 1 < len(terms) else terms[n] for n in range(0, len(terms), 2)]
    return terms[0]


def kernel(
    nx, ny, rows, cols,
    guess, velocity, leaf, canopy, solid, receptors,
    out,
    start, basis, packed, coef, raw_vel, raw_leaf, raw_canopy, raw_solid,
    halves, gram, mine, plane_in, line, line_in, aims,
    load_sem, halo_send, halo_recv, plane_send, plane_recv, line_send, line_recv, met_x, met_y,
):
    gx = lax.axis_index("gx")
    gy = lax.axis_index("gy")

    def peer(dx, dy):
        return {
            "gx": lax.rem(gx + dx + nx, nx) if dx else gx,
            "gy": lax.rem(gy + dy + ny, ny) if dy else gy,
        }

    def inside(dy):
        return jnp.logical_and(gy + dy >= 0, gy + dy < ny)

    def where_inside(dy, act):
        if dy:
            pl.when(inside(dy))(act)
        else:
            act()

    def signal(sem, side):
        where_inside(
            side[1],
            lambda: pl.semaphore_signal(sem, inc=1, device_id=peer(*side), device_id_type=pl.DeviceIdType.MESH),
        )

    def both(d):
        return inside(d).astype(jnp.int32) + inside(-d).astype(jnp.int32)

    barrier = pltpu.get_barrier_semaphore()
    for side in SIDES:
        signal(barrier, side)

    def rounds(most):
        reach, out = 1, []
        while reach < most:
            out.append(reach)
            reach *= 2
        return out

    rounds_x, rounds_y = rounds(nx // 2), rounds(ny - 1)

    def tell_x(n):
        if n < len(rounds_x):
            for d in (rounds_x[n], -rounds_x[n]):
                signal(met_x.at[n], (d, 0))

    def tell_y(n):
        if n < len(rounds_y):
            for d in (rounds_y[n], -rounds_y[n]):
                signal(met_y.at[n], (0, d))

    def pass_x(n):
        if n < len(rounds_x):
            pl.semaphore_wait(met_x.at[n], 2)
            tell_x(n + 1)

    def pass_y(n):
        if n < len(rounds_y):
            pl.semaphore_wait(met_y.at[n], both(rounds_y[n]))
            tell_y(n + 1)


    own_r, own_c = pl.ds(PAD_R, rows), pl.ds(PAD_C, cols)
    loads = [
        pltpu.make_async_copy(velocity, raw_vel, load_sem.at[0]),
        pltpu.make_async_copy(leaf, raw_leaf, load_sem.at[1]),
        pltpu.make_async_copy(canopy, raw_canopy, load_sem.at[2]),
        pltpu.make_async_copy(solid, raw_solid, load_sem.at[3]),
        pltpu.make_async_copy(guess, start.at[own_r, own_c], load_sem.at[4]),
        pltpu.make_async_copy(receptors, aims, load_sem.at[5]),
    ]
    for copy in loads:
        copy.start()

    def clear(side):
        for ref in (start, packed, basis.at[FIRST - 1]):
            ref[:, side, :] = jnp.zeros((ref.shape[0], PAD_C, ref.shape[2]), jnp.float32)

    pl.when(gy == 0)(lambda: clear(slice(0, PAD_C)))
    pl.when(gy == ny - 1)(lambda: clear(slice(PAD_C + cols, 2 * PAD_C + cols)))

    sub = lax.broadcasted_iota(jnp.int32, (8, LANES), 0)
    lane = lax.broadcasted_iota(jnp.int32, (8, LANES), 1)

    for copy in loads[:4]:
        copy.wait()
    reaction = penalty * raw_solid[...].astype(jnp.float32) + leaf_gain * raw_leaf[...] * raw_canopy[...].astype(jnp.float32)
    parts = [raw_vel[0], raw_vel[1], raw_vel[2], reaction]
    spread = (sub % 4) * NZ + lane % NZ
    for i in range(rows):
        for tile in range(cols // 8):
            total = None
            for n, part in enumerate(parts):
                low = jnp.broadcast_to(part[i : i + 1, (2 * tile) * LANES : (2 * tile + 1) * LANES], (8, LANES))
                high = jnp.broadcast_to(part[i : i + 1, (2 * tile + 1) * LANES : (2 * tile + 2) * LANES], (8, LANES))
                value = jnp.take_along_axis(jnp.where(sub < 4, low, high), spread, axis=1)
                total = value if total is None else jnp.where(lane // NZ == n, value, total)
            packed[PAD_R + i, PAD_C + 8 * tile : PAD_C + 8 * tile + 8, :] = total

    for copy in loads[4:]:
        copy.wait()
    pl.semaphore_wait(barrier, 3 * (1 + both(1)) - 1)

    reach = max(FIRST - 1, DEGREE - FIRST)

    def exchange(ref, bank, reach):
        copies = []
        for n, (dx, dy) in enumerate(SIDES):
            near = reach - 1 if dx and dy else reach
            src_r, dst_r = window(dx, near, rows, PAD_R)
            src_c, dst_c = window(dy, near, cols, PAD_C)
            copies.append(
                (
                    dy,
                    pltpu.make_async_remote_copy(
                        src_ref=ref.at[src_r, src_c],
                        dst_ref=ref.at[dst_r, dst_c],
                        send_sem=halo_send.at[bank, n],
                        recv_sem=halo_recv.at[bank, n],
                        device_id=peer(dx, dy),
                        device_id_type=pl.DeviceIdType.MESH,
                    ),
                )
            )
        for dy, copy in copies:
            where_inside(dy, copy.start)
        return copies

    def arrive(copies):
        for dy, copy in copies:
            where_inside(-dy, copy.wait_recv)

    moving_0 = exchange(packed, 0, reach)
    moving_1 = exchange(start, 1, FIRST)
    tell_x(0)
    tell_y(0)

    inv = 1.0 / SCALE
    first_row = jnp.where(gx == 0, 0.0, inv)
    last_row = jnp.where(gx == nx - 1, 0.0, inv)
    first_col = jnp.where(gy == 0, 0.0, inv)
    last_col = jnp.where(gy == ny - 1, 0.0, inv)
    tiles = (cols + 2 * PAD_C) // 8
    first_tile, last_tile = PAD_C // 8, (PAD_C + cols) // 8 - 1
    own_cells = [(r, tile) for r in range(PAD_R, PAD_R + rows) for tile in range(first_tile, last_tile + 1)]
    all_cells = [
        (r, tile)
        for r in range(PAD_R - reach, PAD_R + rows + reach)
        for tile in range(tiles)
        if PAD_R - reach < r < PAD_R + rows + reach - 1 or first_tile <= tile <= last_tile
    ]

    def expand(cells):
        for r, tile in cells:
            here = pl.ds(8 * tile, 8)
            cell = packed[r, 8 * tile : 8 * tile + 8, :]
            for half in range(2):
                span = slice(half * LANES, (half + 1) * LANES)
                level = lane // R + half * (LANES // R)
                u, v, w, react = (jnp.take_along_axis(cell, n * NZ + level, axis=1) for n in range(4))
                relu = lambda value: jnp.maximum(value, 0.0)
                east, west = horiz_diff + relu(u), horiz_diff + relu(-u)
                north, south = horiz_diff + relu(v), horiz_diff + relu(-v)
                up, down = vert_diff + relu(w), vert_diff + relu(-w)
                diag = decay_rate + react + east + west + north + south + up + down
                coef[0, r, here, span] = (diag - SHIFT) * inv
                coef[1, r, here, span] = east * (last_row if r == PAD_R + rows - 1 else inv)
                coef[2, r, here, span] = west * (first_row if r == PAD_R else inv)
                coef[3, r, here, span] = north * (jnp.where(sub == 7, last_col, inv) if tile == last_tile else inv)
                coef[4, r, here, span] = south * (jnp.where(sub == 0, first_col, inv) if tile == first_tile else inv)
                coef[5, r, here, span] = up * (jnp.where(lane >= LANES - R, 0.0, inv) if half else inv)
                coef[6, r, here, span] = down * (inv if half else jnp.where(lane < R, 0.0, inv))

    expand(own_cells)
    pass_x(0)
    pass_y(0)
    arrive(moving_0)
    expand([cell for cell in all_cells if cell not in own_cells])
    pass_y(1)
    arrive(moving_1)
    pass_x(1)

    def apply(ref, r, inner):
        height = cols + 2 * PAD_C
        width = NZ * R
        cut = slice(PAD_C, PAD_C + cols) if inner else slice(0, height)
        centre = ref[r]
        north = pltpu.roll(centre, height - 1, 0)[cut]
        south = pltpu.roll(centre, 1, 0)[cut]
        middle = centre[cut]
        up = pltpu.roll(middle, width - R, 1)
        down = pltpu.roll(middle, R, 1)
        return (
            coef[0, r, cut, :] * middle
            - coef[1, r, cut, :] * ref[r + 1, cut, :]
            - coef[2, r, cut, :] * ref[r - 1, cut, :]
            - coef[3, r, cut, :] * north
            - coef[4, r, cut, :] * south
            - coef[5, r, cut, :] * up
            - coef[6, r, cut, :] * down
        )

    height = cols + 2 * PAD_C
    lanes = lax.broadcasted_iota(jnp.int32, (height, NZ * R), 1)
    place = lax.broadcasted_iota(jnp.int32, (height, NZ * R), 0) + (gy * cols - PAD_C)
    aim = jnp.full((height, NZ * R), -1 << 30, jnp.int32)
    for q in range(R):
        aim = jnp.where(lanes == R + q, aims[q], aim)
    aim = aim - place
    for r in range(PAD_R - FIRST + 1, PAD_R + rows + FIRST - 1):
        source = jnp.where(aim == (gx * rows + (r - PAD_R)) * (ny * cols), source_gain, 0.0)
        basis[0, r] = source - (SCALE * apply(start, r, False) + SHIFT * start[r])

    def advance(j, reach):
        for r in range(PAD_R - reach, PAD_R + rows + reach):
            if reach:
                basis[j, r] = apply(basis.at[j - 1], r, False)
            else:
                basis[j, r, PAD_C : PAD_C + cols, :] = apply(basis.at[j - 1], r, True)

    def products(a):
        spots = [
            (r, c, half)
            for r in range(PAD_R, PAD_R + rows)
            for c in range(PAD_C, PAD_C + cols, 8)
            for half in range(2)
        ]
        for b in range(a + 1):
            sums[a, b] = None
        for n, (r, c, half) in enumerate(spots):
            high, low = split(basis[a, r, c : c + 8, half * LANES : (half + 1) * LANES])
            halves[a, n, 0], halves[a, n, 1] = high, low
            for b in range(a + 1):
                if b == a:
                    exact, cross, rest = high * high, 2.0 * (high * low), low * low
                else:
                    high_b, low_b = halves[b, n, 0], halves[b, n, 1]
                    exact, cross, rest = high * high_b, high * low_b + low * high_b, low * low_b
                if sums[a, b] is None:
                    sums[a, b] = (exact, cross + rest)
                else:
                    total, error = two_sum(sums[a, b][0], exact)
                    sums[a, b] = (total, sums[a, b][1] + (error + (cross + rest)))

    def turn(value, shift, axis):
        return pltpu.roll(value, shift % value.shape[axis], axis)

    def weave(x, y, bit, axis):
        low = ((sub if axis == 0 else lane) & bit) == 0
        near = tuple(jnp.where(low, u, v) for u, v in zip(x, y))
        far = tuple(jnp.where(low, turn(u, -bit, axis), turn(v, bit, axis)) for u, v in zip(x, y))
        return pair_add(near, far)

    def stack(pairs):
        zero = jnp.zeros((8, LANES), jnp.float32)
        got = [sums[pair] if pair else (zero, zero) for pair in pairs]
        for bit in (4, 2, 1):
            got = [weave(got[n], got[n + bit], bit, 0) for n in range(bit)]
        return got[0]

    sums = {}
    blocks = [PAIRS[n : n + 8] for n in range(0, len(PAIRS), 8)]
    blocks[-1] += [None] * (8 - len(blocks[-1]))
    for j in range(1, FIRST):
        advance(j, FIRST - 1 - j)
    moving_2 = exchange(basis.at[FIRST - 1], 2, DEGREE + 1 - FIRST)
    for a in range(FIRST):
        products(a)
    stacked = [stack(block) for block in blocks if block[-1] and block[-1][0] < FIRST]
    pass_y(2)
    arrive(moving_2)
    pass_x(2)
    pass_y(3)
    for j in range(FIRST, DEGREE + 1):
        advance(j, DEGREE - j)
        products(j)
    stacked += [stack(block) for block in blocks[len(stacked) :]]

    quarter = [weave(stacked[n], stacked[n + 2], 64, 1) for n in range(2)]
    folded = weave(quarter[0], quarter[1], 32, 1)
    folded = weave(folded, folded, 16, 1)
    folded = weave(folded, folded, 8, 1)
    chosen = (lane // R) % 4 == sub % 4
    for n, value in enumerate(folded):
        value = jnp.where(chosen, value, 0.0)
        mine[n, 0:1, :] = jnp.sum(value[0:4], axis=0, keepdims=True)
        mine[n, 1:2, :] = jnp.sum(value[4:8], axis=0, keepdims=True)

    def gather(src, dst, index, count, send_sem, recv_sem, to):
        copies = [
            pltpu.make_async_remote_copy(
                src_ref=src,
                dst_ref=dst.at[index],
                send_sem=send_sem,
                recv_sem=recv_sem,
                device_id=to(d),
                device_id_type=pl.DeviceIdType.MESH,
            )
            for d in sorted(range(1, count), key=lambda d: -min(d, count - d))
        ]
        for copy in copies:
            copy.start()
        dst[index] = src[...]
        some = dst.at[pl.ds(0, count - 1)]
        pltpu.make_async_copy(some, some, recv_sem).wait()
        total = tree([(dst[n, 0], dst[n, 1]) for n in range(count)], pair_add)
        return total, pltpu.make_async_copy(some, some, send_sem)

    for n in range(3, len(rounds_x)):
        pass_x(n)
    line_sum, line_left = gather(mine, line_in, gx, nx, line_send, line_recv, lambda d: peer(d, 0))
    line[0], line[1] = line_sum
    for n in range(4, len(rounds_y)):
        pass_y(n)
    total, plane_left = gather(line, plane_in, gy, ny, plane_send, plane_recv, lambda d: peer(0, d))

    value, error = total
    value, error = two_sum(value, error)
    upper = sub < 4
    for z in range(4):
        index = 32 * z + R * (sub % 4) + lane % R
        spread_out = lambda x: jnp.take_along_axis(
            jnp.where(upper, jnp.broadcast_to(x[0:1], (8, LANES)), jnp.broadcast_to(x[1:2], (8, LANES))), index, axis=1
        )
        here = spread_out(value)
        gram[0, 8 * z : 8 * z + 8, :] = here
        gram[1, 8 * z : 8 * z + 8, :] = spread_out(error)
        gram[2, 8 * z : 8 * z + 8, :], gram[3, 8 * z : 8 * z + 8, :] = split(here)

    def product(a, b):
        whole, high, low = b
        top = a[0] * whole
        return top, (((a[2] * high - top) + a[2] * low + a[3] * high) + a[3] * low) + a[1] * whole

    def entry(i, j):
        n = SLOT[max(i, j), min(i, j)]
        return tuple(gram[k, n : n + 1, :] for k in range(4))

    def with_halves(values):
        return [(value,) + split(value) for value in values]

    def pull(values, count):
        out = []
        for i in range(count):
            total, error = tree([product(entry(i, j), value) for j, value in enumerate(values)], pair_add)
            total, error = two_sum(total, error)
            out.append((total, error) + split(total))
        return out

    def inner(pulled, values):
        total, error = tree([product(a, b) for a, b in zip(pulled, values)], pair_add)
        return total + error

    shift = SHIFT / SCALE

    def operate(d):
        out = []
        for j in range(len(d) + 1):
            terms = ([shift * d[j]] if j < len(d) else []) + ([d[j - 1]] if j else [])
            out.append(terms[0] if len(terms) == 1 else terms[0] + terms[1])
        return out

    d = [jnp.ones((1, LANES), jnp.float32)]
    y = [jnp.zeros((1, LANES), jnp.float32) for _ in range(DEGREE)]
    for _ in range(CYCLES):
        image = operate(d)
        held, moved = with_halves(d), with_halves(image)
        pulled = pull(held, len(image))
        alpha = inner(pulled, held) / inner(pulled, moved)
        half_way = [(d[i] - alpha * image[i]) if i < len(d) else -(alpha * image[i]) for i in range(len(image))]
        turned = operate(half_way)
        held, moved = with_halves(half_way), with_halves(turned)
        pulled = pull(moved, len(turned))
        omega = inner(pulled, held) / inner(pulled, moved)
        for i in range(len(d)):
            y[i] = y[i] + alpha * d[i]
        for i in range(len(half_way)):
            y[i] = y[i] + omega * half_way[i]
        d = [
            (half_way[i] - omega * turned[i]) if i < len(half_way) else -(omega * turned[i])
            for i in range(len(turned))
        ]

    steps = [value * inv for value in y]
    for r in range(rows):
        for c in range(0, cols, 8):
            for half in range(2):
                span = slice(half * LANES, (half + 1) * LANES)
                held = [basis[j, PAD_R + r, PAD_C + c : PAD_C + c + 8, span] for j in range(DEGREE + 1)]
                moved = tree([steps[j] * held[j] for j in range(DEGREE)], jnp.add)
                out[0, r, c : c + 8, span] = start[PAD_R + r, PAD_C + c : PAD_C + c + 8, span] + moved
                out[1, r, c : c + 8, span] = tree([d[j] * held[j] for j in range(DEGREE + 1)], jnp.add)

    for dy, copy in moving_0 + moving_1 + moving_2:
        where_inside(dy, copy.wait_send)
    plane_left.wait()
    line_left.wait()


def solution(mesh):
    nx, ny = mesh.shape["gx"], mesh.shape["gy"]

    def body(*arrays):
        adjoint_guess, velocity, leaf_rate, canopy, solid, receptors = arrays
        rows, cols = adjoint_guess.shape[0], adjoint_guess.shape[1]
        tall, wide = rows + 2 * PAD_R, cols + 2 * PAD_C
        shape = jax.ShapeDtypeStruct((2,) + adjoint_guess.shape, jnp.float32)
        both = pl.pallas_call(
            functools.partial(kernel, nx, ny, rows, cols),
            out_shape=shape,
            in_specs=[pl.BlockSpec(memory_space=pltpu.HBM)] * 6,
            out_specs=pl.BlockSpec(memory_space=pltpu.VMEM),
            scratch_shapes=[
                pltpu.VMEM((tall, wide, NZ * R), jnp.float32),
                pltpu.VMEM((DEGREE + 1, tall, wide, NZ * R), jnp.float32),
                pltpu.VMEM((tall, wide, LANES), jnp.float32),
                pltpu.VMEM((7, tall, wide, NZ * R), jnp.float32),
                pltpu.VMEM(velocity.shape, jnp.float32),
                pltpu.VMEM(leaf_rate.shape, jnp.float32),
                pltpu.VMEM(canopy.shape, jnp.int32),
                pltpu.VMEM(solid.shape, jnp.int32),
                pltpu.VMEM((DEGREE + 1, rows * cols * 2 // 8, 2, 8, LANES), jnp.float32),
                pltpu.VMEM((4, 32, LANES), jnp.float32),
                pltpu.VMEM((2, 2, LANES), jnp.float32),
                pltpu.VMEM((ny, 2, 2, LANES), jnp.float32),
                pltpu.VMEM((2, 2, LANES), jnp.float32),
                pltpu.VMEM((nx, 2, 2, LANES), jnp.float32),
                pltpu.SMEM(receptors.shape, jnp.int32),
                pltpu.SemaphoreType.DMA((6,)),
                pltpu.SemaphoreType.DMA((3, len(SIDES))),
                pltpu.SemaphoreType.DMA((3, len(SIDES))),
                pltpu.SemaphoreType.DMA,
                pltpu.SemaphoreType.DMA,
                pltpu.SemaphoreType.DMA,
                pltpu.SemaphoreType.DMA,
                pltpu.SemaphoreType.REGULAR((8,)),
                pltpu.SemaphoreType.REGULAR((8,)),
            ],
            compiler_params=pltpu.CompilerParams(collective_id=0, has_side_effects=True, vmem_limit_bytes=16 << 20),
        )(*(pltpu.with_memory_space_constraint(array, pltpu.HBM) for array in arrays))
        return both[0], both[1]

    return jax.shard_map(
        body,
        mesh=mesh,
        in_specs=(
            P("gx", "gy", None),
            P(None, "gx", "gy"),
            P("gx", "gy"),
            P("gx", "gy"),
            P("gx", "gy"),
            P(),
        ),
        out_specs=(P("gx", "gy", None), P("gx", "gy", None)),
        check_vma=False,
    )
```

```python
import functools

import jax
import jax.numpy as jnp
from jax import lax
from jax.experimental import pallas as pl
from jax.experimental.pallas import tpu as pltpu
from jax.sharding import PartitionSpec as P

NZ = 32
R = 8
CYCLES = 3
DEGREE = 2 * CYCLES

horiz_diff = 4.0
vert_diff = 2.0
decay_rate = 3.5
penalty = 40.0
leaf_gain = 4.0
source_gain = 32.0

SHIFT = 27.0
SCALE = 16.0

FIRST = 4
PAD_R = 4
PAD_C = 8
LANES = 128

PAIRS = [(a, b) for a in range(DEGREE + 1) for b in range(a + 1)]
SLOT = {pair: n for n, pair in enumerate(PAIRS)}
SIDES = [(1, 1), (1, -1), (-1, 1), (-1, -1), (0, 1), (0, -1), (1, 0), (-1, 0)]


def window(delta, reach, own, pad):
    if delta == 0:
        return pl.ds(pad, own), pl.ds(pad, own)
    if delta > 0:
        return pl.ds(pad + own - reach, reach), pl.ds(pad - reach, reach)
    return pl.ds(pad, reach), pl.ds(pad + own, reach)


def two_sum(a, b):
    total = a + b
    back = total - a
    return total, (a - (total - back)) + (b - back)


def pair_add(a, b):
    total, error = two_sum(a[0], b[0])
    return total, error + (a[1] + b[1])


def split(value):
    scaled = value * 4097.0
    high = scaled - (scaled - value)
    return high, value - high


def tree(terms, join):
    terms = list(terms)
    while len(terms) > 1:
        terms = [join(terms[n], terms[n + 1]) if n + 1 < len(terms) else terms[n] for n in range(0, len(terms), 2)]
    return terms[0]


def kernel(
    nx, ny, rows, cols,
    guess, velocity, leaf, canopy, solid, receptors,
    out,
    start, basis, packed, coef, raw_vel, raw_leaf, raw_canopy, raw_solid,
    halves, gram, mine, plane_in, line, line_in, aims,
    load_sem, halo_send, halo_recv, plane_send, plane_recv, line_send, line_recv, met_x, met_y,
):
    gx = lax.axis_index("gx")
    gy = lax.axis_index("gy")

    def peer(dx, dy):
        return {
            "gx": lax.rem(gx + dx + nx, nx) if dx else gx,
            "gy": lax.rem(gy + dy + ny, ny) if dy else gy,
        }

    def inside(dy):
        return jnp.logical_and(gy + dy >= 0, gy + dy < ny)

    def where_inside(dy, act):
        if dy:
            pl.when(inside(dy))(act)
        else:
            act()

    def signal(sem, side):
        where_inside(
            side[1],
            lambda: pl.semaphore_signal(sem, inc=1, device_id=peer(*side), device_id_type=pl.DeviceIdType.MESH),
        )

    def both(d):
        return inside(d).astype(jnp.int32) + inside(-d).astype(jnp.int32)

    barrier = pltpu.get_barrier_semaphore()
    for side in SIDES:
        signal(barrier, side)

    def rounds(most):
        reach, out = 1, []
        while reach < most:
            out.append(reach)
            reach *= 2
        return out

    rounds_x, rounds_y = rounds(nx // 2), rounds(ny - 1)

    def tell_x(n):
        if n < len(rounds_x):
            for d in (rounds_x[n], -rounds_x[n]):
                signal(met_x.at[n], (d, 0))

    def tell_y(n):
        if n < len(rounds_y):
            for d in (rounds_y[n], -rounds_y[n]):
                signal(met_y.at[n], (0, d))

    def pass_x(n):
        if n < len(rounds_x):
            pl.semaphore_wait(met_x.at[n], 2)
            tell_x(n + 1)

    def pass_y(n):
        if n < len(rounds_y):
            pl.semaphore_wait(met_y.at[n], both(rounds_y[n]))
            tell_y(n + 1)


    own_r, own_c = pl.ds(PAD_R, rows), pl.ds(PAD_C, cols)
    loads = [
        pltpu.make_async_copy(velocity, raw_vel, load_sem.at[0]),
        pltpu.make_async_copy(leaf, raw_leaf, load_sem.at[1]),
        pltpu.make_async_copy(canopy, raw_canopy, load_sem.at[2]),
        pltpu.make_async_copy(solid, raw_solid, load_sem.at[3]),
        pltpu.make_async_copy(guess, start.at[own_r, own_c], load_sem.at[4]),
        pltpu.make_async_copy(receptors, aims, load_sem.at[5]),
    ]
    for copy in loads:
        copy.start()

    def clear(side):
        for ref in (start, packed, basis.at[FIRST - 1]):
            ref[:, side, :] = jnp.zeros((ref.shape[0], PAD_C, ref.shape[2]), jnp.float32)

    pl.when(gy == 0)(lambda: clear(slice(0, PAD_C)))
    pl.when(gy == ny - 1)(lambda: clear(slice(PAD_C + cols, 2 * PAD_C + cols)))

    sub = lax.broadcasted_iota(jnp.int32, (8, LANES), 0)
    lane = lax.broadcasted_iota(jnp.int32, (8, LANES), 1)

    for copy in loads[:4]:
        copy.wait()
    reaction = penalty * raw_solid[...].astype(jnp.float32) + leaf_gain * raw_leaf[...] * raw_canopy[...].astype(jnp.float32)
    parts = [raw_vel[0], raw_vel[1], raw_vel[2], reaction]
    spread = (sub % 4) * NZ + lane % NZ
    for i in range(rows):
        for tile in range(cols // 8):
            total = None
            for n, part in enumerate(parts):
                low = jnp.broadcast_to(part[i : i + 1, (2 * tile) * LANES : (2 * tile + 1) * LANES], (8, LANES))
                high = jnp.broadcast_to(part[i : i + 1, (2 * tile + 1) * LANES : (2 * tile + 2) * LANES], (8, LANES))
                value = jnp.take_along_axis(jnp.where(sub < 4, low, high), spread, axis=1)
                total = value if total is None else jnp.where(lane // NZ == n, value, total)
            packed[PAD_R + i, PAD_C + 8 * tile : PAD_C + 8 * tile + 8, :] = total

    for copy in loads[4:]:
        copy.wait()
    pl.semaphore_wait(barrier, 3 * (1 + both(1)) - 1)

    reach = max(FIRST - 1, DEGREE - FIRST)

    def exchange(ref, bank, reach):
        copies = []
        for n, (dx, dy) in enumerate(SIDES):
            near = reach - 1 if dx and dy else reach
            src_r, dst_r = window(dx, near, rows, PAD_R)
            src_c, dst_c = window(dy, near, cols, PAD_C)
            copies.append(
                (
                    dy,
                    pltpu.make_async_remote_copy(
                        src_ref=ref.at[src_r, src_c],
                        dst_ref=ref.at[dst_r, dst_c],
                        send_sem=halo_send.at[bank, n],
                        recv_sem=halo_recv.at[bank, n],
                        device_id=peer(dx, dy),
                        device_id_type=pl.DeviceIdType.MESH,
                    ),
                )
            )
        for dy, copy in copies:
            where_inside(dy, copy.start)
        return copies

    def arrive(copies):
        for dy, copy in copies:
            where_inside(-dy, copy.wait_recv)

    moving_0 = exchange(packed, 0, reach)
    moving_1 = exchange(start, 1, FIRST)
    tell_x(0)
    tell_y(0)

    inv = 1.0 / SCALE
    first_row = jnp.where(gx == 0, 0.0, inv)
    last_row = jnp.where(gx == nx - 1, 0.0, inv)
    first_col = jnp.where(gy == 0, 0.0, inv)
    last_col = jnp.where(gy == ny - 1, 0.0, inv)
    tiles = (cols + 2 * PAD_C) // 8
    first_tile, last_tile = PAD_C // 8, (PAD_C + cols) // 8 - 1
    own_cells = [(r, tile) for r in range(PAD_R, PAD_R + rows) for tile in range(first_tile, last_tile + 1)]
    all_cells = [
        (r, tile)
        for r in range(PAD_R - reach, PAD_R + rows + reach)
        for tile in range(tiles)
        if PAD_R - reach < r < PAD_R + rows + reach - 1 or first_tile <= tile <= last_tile
    ]

    def expand(cells):
        for r, tile in cells:
            here = pl.ds(8 * tile, 8)
            cell = packed[r, 8 * tile : 8 * tile + 8, :]
            for half in range(2):
                span = slice(half * LANES, (half + 1) * LANES)
                level = lane // R + half * (LANES // R)
                u, v, w, react = (jnp.take_along_axis(cell, n * NZ + level, axis=1) for n in range(4))
                relu = lambda value: jnp.maximum(value, 0.0)
                east, west = horiz_diff + relu(u), horiz_diff + relu(-u)
                north, south = horiz_diff + relu(v), horiz_diff + relu(-v)
                up, down = vert_diff + relu(w), vert_diff + relu(-w)
                diag = decay_rate + react + east + west + north + south + up + down
                coef[0, r, here, span] = (diag - SHIFT) * inv
                coef[1, r, here, span] = east * (last_row if r == PAD_R + rows - 1 else inv)
                coef[2, r, here, span] = west * (first_row if r == PAD_R else inv)
                coef[3, r, here, span] = north * (jnp.where(sub == 7, last_col, inv) if tile == last_tile else inv)
                coef[4, r, here, span] = south * (jnp.where(sub == 0, first_col, inv) if tile == first_tile else inv)
                coef[5, r, here, span] = up * (jnp.where(lane >= LANES - R, 0.0, inv) if half else inv)
                coef[6, r, here, span] = down * (inv if half else jnp.where(lane < R, 0.0, inv))

    expand(own_cells)
    pass_x(0)
    pass_y(0)
    arrive(moving_0)
    expand([cell for cell in all_cells if cell not in own_cells])
    pass_y(1)
    arrive(moving_1)
    pass_x(1)

    def apply(ref, r, cut):
        height = cols + 2 * PAD_C
        width = NZ * R
        centre = ref[r]
        north = pltpu.roll(centre, height - 1, 0)[cut]
        south = pltpu.roll(centre, 1, 0)[cut]
        middle = centre[cut]
        up = pltpu.roll(middle, width - R, 1)
        down = pltpu.roll(middle, R, 1)
        return (
            coef[0, r, cut, :] * middle
            - coef[1, r, cut, :] * ref[r + 1, cut, :]
            - coef[2, r, cut, :] * ref[r - 1, cut, :]
            - coef[3, r, cut, :] * north
            - coef[4, r, cut, :] * south
            - coef[5, r, cut, :] * up
            - coef[6, r, cut, :] * down
        )

    height = cols + 2 * PAD_C
    lanes = lax.broadcasted_iota(jnp.int32, (height, NZ * R), 1)
    place = lax.broadcasted_iota(jnp.int32, (height, NZ * R), 0) + (gy * cols - PAD_C)
    aim = jnp.full((height, NZ * R), -1 << 30, jnp.int32)
    for q in range(R):
        aim = jnp.where(lanes == R + q, aims[q], aim)
    aim = aim - place
    for r in range(PAD_R - FIRST + 1, PAD_R + rows + FIRST - 1):
        source = jnp.where(aim == (gx * rows + (r - PAD_R)) * (ny * cols), source_gain, 0.0)
        cut = slice(PAD_C, PAD_C + cols) if r in (PAD_R - FIRST + 1, PAD_R + rows + FIRST - 2) else slice(0, height)
        basis[0, r, cut, :] = source[cut] - (SCALE * apply(start, r, cut) + SHIFT * start[r, cut, :])

    def advance(j, reach):
        for r in range(PAD_R - reach, PAD_R + rows + reach):
            outer = reach == 0 or r in (PAD_R - reach, PAD_R + rows + reach - 1)
            cut = slice(PAD_C, PAD_C + cols) if outer else slice(0, height)
            basis[j, r, cut, :] = apply(basis.at[j - 1], r, cut)

    def products(a):
        spots = [
            (r, c, half)
            for r in range(PAD_R, PAD_R + rows)
            for c in range(PAD_C, PAD_C + cols, 8)
            for half in range(2)
        ]
        values = [basis[a, r, c : c + 8, half * LANES : (half + 1) * LANES] for r, c, half in spots]
        peaks[a] = tree([jnp.abs(value) for value in values], jnp.maximum)
        anchors = [(4.0 * len(spots)) * (peaks[a] * peaks[b]) for b in range(a + 1)]
        totals, errors = list(anchors), [None] * (a + 1)
        for n, value in enumerate(values):
            high, low = split(value)
            halves[a, n, 0], halves[a, n, 1] = high, low
            for b in range(a + 1):
                high_b, low_b = (high, low) if b == a else (halves[b, n, 0], halves[b, n, 1])
                exact = high * high_b
                small = high * low_b + low * (high_b + low_b)
                total = totals[b] + exact
                small = small + (exact - (total - totals[b]))
                totals[b], errors[b] = total, small if n == 0 else errors[b] + small
        for b in range(a + 1):
            sums[a, b] = (totals[b] - anchors[b], errors[b])

    def turn(value, shift, axis):
        return pltpu.roll(value, shift % value.shape[axis], axis)

    def weave(x, y, bit, axis):
        low = ((sub if axis == 0 else lane) & bit) == 0
        near = tuple(jnp.where(low, u, v) for u, v in zip(x, y))
        far = tuple(jnp.where(low, turn(u, -bit, axis), turn(v, bit, axis)) for u, v in zip(x, y))
        return pair_add(near, far)

    def stack(pairs):
        zero = jnp.zeros((8, LANES), jnp.float32)
        got = [sums[pair] if pair else (zero, zero) for pair in pairs]
        for bit in (4, 2, 1):
            got = [weave(got[n], got[n + bit], bit, 0) for n in range(bit)]
        return got[0]

    sums, peaks = {}, {}
    blocks = [PAIRS[n : n + 8] for n in range(0, len(PAIRS), 8)]
    blocks[-1] += [None] * (8 - len(blocks[-1]))
    for j in range(1, FIRST):
        advance(j, FIRST - 1 - j)
    moving_2 = exchange(basis.at[FIRST - 1], 2, DEGREE + 1 - FIRST)
    for a in range(FIRST):
        products(a)
    stacked = [stack(block) for block in blocks if block[-1] and block[-1][0] < FIRST]
    pass_y(2)
    arrive(moving_2)
    pass_x(2)
    pass_y(3)
    for j in range(FIRST, DEGREE + 1):
        advance(j, DEGREE - j)
        products(j)
    stacked += [stack(block) for block in blocks[len(stacked) :]]

    quarter = [weave(stacked[n], stacked[n + 2], 64, 1) for n in range(2)]
    folded = weave(quarter[0], quarter[1], 32, 1)
    folded = weave(folded, folded, 16, 1)
    folded = weave(folded, folded, 8, 1)
    chosen = (lane // R) % 4 == sub % 4
    for n, value in enumerate(folded):
        value = jnp.where(chosen, value, 0.0)
        mine[n, 0:1, :] = jnp.sum(value[0:4], axis=0, keepdims=True)
        mine[n, 1:2, :] = jnp.sum(value[4:8], axis=0, keepdims=True)

    def gather(src, dst, index, count, send_sem, recv_sem, to):
        copies = [
            pltpu.make_async_remote_copy(
                src_ref=src,
                dst_ref=dst.at[index],
                send_sem=send_sem,
                recv_sem=recv_sem,
                device_id=to(d),
                device_id_type=pl.DeviceIdType.MESH,
            )
            for d in sorted(range(1, count), key=lambda d: -min(d, count - d))
        ]
        for copy in copies:
            copy.start()
        dst[index] = src[...]
        some = dst.at[pl.ds(0, count - 1)]
        pltpu.make_async_copy(some, some, recv_sem).wait()
        total = tree([(dst[n, 0], dst[n, 1]) for n in range(count)], pair_add)
        return total, pltpu.make_async_copy(some, some, send_sem)

    for n in range(3, len(rounds_x)):
        pass_x(n)
    line_sum, line_left = gather(mine, line_in, gx, nx, line_send, line_recv, lambda d: peer(d, 0))
    line[0], line[1] = line_sum
    for n in range(4, len(rounds_y)):
        pass_y(n)
    total, plane_left = gather(line, plane_in, gy, ny, plane_send, plane_recv, lambda d: peer(0, d))

    value, error = total
    value, error = two_sum(value, error)
    upper = sub < 4
    for z in range(4):
        index = 32 * z + R * (sub % 4) + lane % R
        spread_out = lambda x: jnp.take_along_axis(
            jnp.where(upper, jnp.broadcast_to(x[0:1], (8, LANES)), jnp.broadcast_to(x[1:2], (8, LANES))), index, axis=1
        )
        here = spread_out(value)
        gram[0, 8 * z : 8 * z + 8, :] = here
        gram[1, 8 * z : 8 * z + 8, :] = spread_out(error)
        gram[2, 8 * z : 8 * z + 8, :], gram[3, 8 * z : 8 * z + 8, :] = split(here)

    def product(a, b):
        whole, high, low = b
        top = a[0] * whole
        return top, (((a[2] * high - top) + a[2] * low + a[3] * high) + a[3] * low) + a[1] * whole

    def entry(i, j):
        n = SLOT[max(i, j), min(i, j)]
        return tuple(gram[k, n : n + 1, :] for k in range(4))

    def with_halves(values):
        return [(value,) + split(value) for value in values]

    def pull(values, count):
        out = []
        for i in range(count):
            total, error = tree([product(entry(i, j), value) for j, value in enumerate(values)], pair_add)
            total, error = two_sum(total, error)
            out.append((total, error) + split(total))
        return out

    def inner(pulled, values):
        total, error = tree([product(a, b) for a, b in zip(pulled, values)], pair_add)
        return total + error

    shift = SHIFT / SCALE

    def operate(d):
        out = []
        for j in range(len(d) + 1):
            terms = ([shift * d[j]] if j < len(d) else []) + ([d[j - 1]] if j else [])
            out.append(terms[0] if len(terms) == 1 else terms[0] + terms[1])
        return out

    d = [jnp.ones((1, LANES), jnp.float32)]
    y = [jnp.zeros((1, LANES), jnp.float32) for _ in range(DEGREE)]
    for _ in range(CYCLES):
        image = operate(d)
        held, moved = with_halves(d), with_halves(image)
        pulled = pull(held, len(image))
        alpha = inner(pulled, held) / inner(pulled, moved)
        half_way = [(d[i] - alpha * image[i]) if i < len(d) else -(alpha * image[i]) for i in range(len(image))]
        turned = operate(half_way)
        held, moved = with_halves(half_way), with_halves(turned)
        pulled = pull(moved, len(turned))
        omega = inner(pulled, held) / inner(pulled, moved)
        for i in range(len(d)):
            y[i] = y[i] + alpha * d[i]
        for i in range(len(half_way)):
            y[i] = y[i] + omega * half_way[i]
        d = [
            (half_way[i] - omega * turned[i]) if i < len(half_way) else -(omega * turned[i])
            for i in range(len(turned))
        ]

    steps = [value * inv for value in y]
    for r in range(rows):
        for c in range(0, cols, 8):
            for half in range(2):
                span = slice(half * LANES, (half + 1) * LANES)
                held = [basis[j, PAD_R + r, PAD_C + c : PAD_C + c + 8, span] for j in range(DEGREE + 1)]
                moved = tree([steps[j] * held[j] for j in range(DEGREE)], jnp.add)
                out[0, r, c : c + 8, span] = start[PAD_R + r, PAD_C + c : PAD_C + c + 8, span] + moved
                out[1, r, c : c + 8, span] = tree([d[j] * held[j] for j in range(DEGREE + 1)], jnp.add)

    for dy, copy in moving_0 + moving_1 + moving_2:
        where_inside(dy, copy.wait_send)
    plane_left.wait()
    line_left.wait()


def solution(mesh):
    nx, ny = mesh.shape["gx"], mesh.shape["gy"]

    def body(*arrays):
        adjoint_guess, velocity, leaf_rate, canopy, solid, receptors = arrays
        rows, cols = adjoint_guess.shape[0], adjoint_guess.shape[1]
        tall, wide = rows + 2 * PAD_R, cols + 2 * PAD_C
        shape = jax.ShapeDtypeStruct((2,) + adjoint_guess.shape, jnp.float32)
        both = pl.pallas_call(
            functools.partial(kernel, nx, ny, rows, cols),
            out_shape=shape,
            in_specs=[pl.BlockSpec(memory_space=pltpu.HBM)] * 6,
            out_specs=pl.BlockSpec(memory_space=pltpu.VMEM),
            scratch_shapes=[
                pltpu.VMEM((tall, wide, NZ * R), jnp.float32),
                pltpu.VMEM((DEGREE + 1, tall, wide, NZ * R), jnp.float32),
                pltpu.VMEM((tall, wide, LANES), jnp.float32),
                pltpu.VMEM((7, tall, wide, NZ * R), jnp.float32),
                pltpu.VMEM(velocity.shape, jnp.float32),
                pltpu.VMEM(leaf_rate.shape, jnp.float32),
                pltpu.VMEM(canopy.shape, jnp.int32),
                pltpu.VMEM(solid.shape, jnp.int32),
                pltpu.VMEM((DEGREE + 1, rows * cols * 2 // 8, 2, 8, LANES), jnp.float32),
                pltpu.VMEM((4, 32, LANES), jnp.float32),
                pltpu.VMEM((2, 2, LANES), jnp.float32),
                pltpu.VMEM((ny, 2, 2, LANES), jnp.float32),
                pltpu.VMEM((2, 2, LANES), jnp.float32),
                pltpu.VMEM((nx, 2, 2, LANES), jnp.float32),
                pltpu.SMEM(receptors.shape, jnp.int32),
                pltpu.SemaphoreType.DMA((6,)),
                pltpu.SemaphoreType.DMA((3, len(SIDES))),
                pltpu.SemaphoreType.DMA((3, len(SIDES))),
                pltpu.SemaphoreType.DMA,
                pltpu.SemaphoreType.DMA,
                pltpu.SemaphoreType.DMA,
                pltpu.SemaphoreType.DMA,
                pltpu.SemaphoreType.REGULAR((8,)),
                pltpu.SemaphoreType.REGULAR((8,)),
            ],
            compiler_params=pltpu.CompilerParams(collective_id=0, has_side_effects=True, vmem_limit_bytes=16 << 20),
        )(*(pltpu.with_memory_space_constraint(array, pltpu.HBM) for array in arrays))
        return both[0], both[1]

    return jax.shard_map(
        body,
        mesh=mesh,
        in_specs=(
            P("gx", "gy", None),
            P(None, "gx", "gy"),
            P("gx", "gy"),
            P("gx", "gy"),
            P("gx", "gy"),
            P(),
        ),
        out_specs=(P("gx", "gy", None), P("gx", "gy", None)),
        check_vma=False,
    )
```

```python
import functools

import jax
import jax.numpy as jnp
from jax import lax
from jax.experimental import pallas as pl
from jax.experimental.pallas import tpu as pltpu
from jax.sharding import PartitionSpec as P

NZ = 32
R = 8
CYCLES = 3
DEGREE = 2 * CYCLES

horiz_diff = 4.0
vert_diff = 2.0
decay_rate = 3.5
penalty = 40.0
leaf_gain = 4.0
source_gain = 32.0

SHIFT = 27.0
SCALE = 16.0

FIRST = 4
PAD_R = 4
PAD_C = 8
LANES = 128

PAIRS = [(a, b) for a in range(DEGREE + 1) for b in range(a + 1)]
SLOT = {pair: n for n, pair in enumerate(PAIRS)}
SIDES = [(1, 1), (1, -1), (-1, 1), (-1, -1), (0, 1), (0, -1), (1, 0), (-1, 0)]


def window(delta, reach, own, pad):
    if delta == 0:
        return pl.ds(pad, own), pl.ds(pad, own)
    if delta > 0:
        return pl.ds(pad + own - reach, reach), pl.ds(pad - reach, reach)
    return pl.ds(pad, reach), pl.ds(pad + own, reach)


def two_sum(a, b):
    total = a + b
    back = total - a
    return total, (a - (total - back)) + (b - back)


def pair_add(a, b):
    total, error = two_sum(a[0], b[0])
    return total, error + (a[1] + b[1])


def split(value):
    scaled = value * 4097.0
    high = scaled - (scaled - value)
    return high, value - high


def tree(terms, join):
    terms = list(terms)
    while len(terms) > 1:
        terms = [join(terms[n], terms[n + 1]) if n + 1 < len(terms) else terms[n] for n in range(0, len(terms), 2)]
    return terms[0]


def kernel(
    nx, ny, rows, cols,
    guess, velocity, leaf, canopy, solid, receptors,
    out,
    start, basis, packed, coef, raw_vel, raw_leaf, raw_canopy, raw_solid,
    halves, gram, mine, plane_in, line, line_in, aims,
    load_sem, halo_send, halo_recv, plane_send, plane_recv, line_send, line_recv, met_x, met_y,
):
    gx = lax.axis_index("gx")
    gy = lax.axis_index("gy")

    def peer(dx, dy):
        return {
            "gx": lax.rem(gx + dx + nx, nx) if dx else gx,
            "gy": lax.rem(gy + dy + ny, ny) if dy else gy,
        }

    def inside(dy):
        return jnp.logical_and(gy + dy >= 0, gy + dy < ny)

    def where_inside(dy, act):
        if dy:
            pl.when(inside(dy))(act)
        else:
            act()

    def signal(sem, side):
        where_inside(
            side[1],
            lambda: pl.semaphore_signal(sem, inc=1, device_id=peer(*side), device_id_type=pl.DeviceIdType.MESH),
        )

    def both(d):
        return inside(d).astype(jnp.int32) + inside(-d).astype(jnp.int32)

    barrier = pltpu.get_barrier_semaphore()
    for side in SIDES:
        signal(barrier, side)

    def rounds(most):
        reach, out = 1, []
        while reach < most:
            out.append(reach)
            reach *= 2
        return out

    rounds_x, rounds_y = rounds(nx // 2), rounds(ny - 1)

    def tell_x(n):
        if n < len(rounds_x):
            for d in (rounds_x[n], -rounds_x[n]):
                signal(met_x.at[n], (d, 0))

    def tell_y(n):
        if n < len(rounds_y):
            for d in (rounds_y[n], -rounds_y[n]):
                signal(met_y.at[n], (0, d))

    def pass_x(n):
        if n < len(rounds_x):
            pl.semaphore_wait(met_x.at[n], 2)
            tell_x(n + 1)

    def pass_y(n):
        if n < len(rounds_y):
            pl.semaphore_wait(met_y.at[n], both(rounds_y[n]))
            tell_y(n + 1)


    own_r, own_c = pl.ds(PAD_R, rows), pl.ds(PAD_C, cols)
    loads = [
        pltpu.make_async_copy(velocity, raw_vel, load_sem.at[0]),
        pltpu.make_async_copy(leaf, raw_leaf, load_sem.at[1]),
        pltpu.make_async_copy(canopy, raw_canopy, load_sem.at[2]),
        pltpu.make_async_copy(solid, raw_solid, load_sem.at[3]),
        pltpu.make_async_copy(guess, start.at[own_r, own_c], load_sem.at[4]),
        pltpu.make_async_copy(receptors, aims, load_sem.at[5]),
    ]
    for copy in loads:
        copy.start()

    def clear(side):
        for ref in (start, packed, basis.at[FIRST - 1]):
            ref[:, side, :] = jnp.zeros((ref.shape[0], PAD_C, ref.shape[2]), jnp.float32)

    pl.when(gy == 0)(lambda: clear(slice(0, PAD_C)))
    pl.when(gy == ny - 1)(lambda: clear(slice(PAD_C + cols, 2 * PAD_C + cols)))

    sub = lax.broadcasted_iota(jnp.int32, (8, LANES), 0)
    lane = lax.broadcasted_iota(jnp.int32, (8, LANES), 1)

    for copy in loads[:4]:
        copy.wait()
    reaction = penalty * raw_solid[...].astype(jnp.float32) + leaf_gain * raw_leaf[...] * raw_canopy[...].astype(jnp.float32)
    parts = [raw_vel[0], raw_vel[1], raw_vel[2], reaction]
    spread = (sub % 4) * NZ + lane % NZ
    for i in range(rows):
        for tile in range(cols // 8):
            total = None
            for n, part in enumerate(parts):
                low = jnp.broadcast_to(part[i : i + 1, (2 * tile) * LANES : (2 * tile + 1) * LANES], (8, LANES))
                high = jnp.broadcast_to(part[i : i + 1, (2 * tile + 1) * LANES : (2 * tile + 2) * LANES], (8, LANES))
                value = jnp.take_along_axis(jnp.where(sub < 4, low, high), spread, axis=1)
                total = value if total is None else jnp.where(lane // NZ == n, value, total)
            packed[PAD_R + i, PAD_C + 8 * tile : PAD_C + 8 * tile + 8, :] = total

    for copy in loads[4:]:
        copy.wait()
    pl.semaphore_wait(barrier, 3 * (1 + both(1)) - 1)

    reach = max(FIRST - 1, DEGREE - FIRST)

    def exchange(ref, bank, reach):
        copies = []
        for n, (dx, dy) in enumerate(SIDES):
            near = reach - 1 if dx and dy else reach
            src_r, dst_r = window(dx, near, rows, PAD_R)
            src_c, dst_c = window(dy, near, cols, PAD_C)
            copies.append(
                (
                    dy,
                    pltpu.make_async_remote_copy(
                        src_ref=ref.at[src_r, src_c],
                        dst_ref=ref.at[dst_r, dst_c],
                        send_sem=halo_send.at[bank, n],
                        recv_sem=halo_recv.at[bank, n],
                        device_id=peer(dx, dy),
                        device_id_type=pl.DeviceIdType.MESH,
                    ),
                )
            )
        return copies

    def depart(copies):
        for dy, copy in copies:
            where_inside(dy, copy.start)

    def arrive(copies):
        for dy, copy in copies:
            where_inside(-dy, copy.wait_recv)

    straight = [n for n, (dx, dy) in enumerate(SIDES) if not dy]
    slanted = [n for n, (dx, dy) in enumerate(SIDES) if dy]

    moving_0 = exchange(packed, 0, reach)
    moving_1 = exchange(start, 1, FIRST)
    for group in (slanted, straight):
        depart([moving_0[n] for n in group])
        depart([moving_1[n] for n in group])
    tell_x(0)
    tell_y(0)

    inv = 1.0 / SCALE
    first_row = jnp.where(gx == 0, 0.0, inv)
    last_row = jnp.where(gx == nx - 1, 0.0, inv)
    first_col = jnp.where(gy == 0, 0.0, inv)
    last_col = jnp.where(gy == ny - 1, 0.0, inv)
    tiles = (cols + 2 * PAD_C) // 8
    first_tile, last_tile = PAD_C // 8, (PAD_C + cols) // 8 - 1
    own_cells = [(r, tile) for r in range(PAD_R, PAD_R + rows) for tile in range(first_tile, last_tile + 1)]
    all_cells = [
        (r, tile)
        for r in range(PAD_R - reach, PAD_R + rows + reach)
        for tile in range(tiles)
        if PAD_R - reach < r < PAD_R + rows + reach - 1 or first_tile <= tile <= last_tile
    ]

    def expand(cells):
        for r, tile in cells:
            here = pl.ds(8 * tile, 8)
            cell = packed[r, 8 * tile : 8 * tile + 8, :]
            for half in range(2):
                span = slice(half * LANES, (half + 1) * LANES)
                level = lane // R + half * (LANES // R)
                u, v, w, react = (jnp.take_along_axis(cell, n * NZ + level, axis=1) for n in range(4))
                relu = lambda value: jnp.maximum(value, 0.0)
                east, west = horiz_diff + relu(u), horiz_diff + relu(-u)
                north, south = horiz_diff + relu(v), horiz_diff + relu(-v)
                up, down = vert_diff + relu(w), vert_diff + relu(-w)
                diag = decay_rate + react + east + west + north + south + up + down
                coef[0, r, here, span] = (diag - SHIFT) * inv
                coef[1, r, here, span] = east * (last_row if r == PAD_R + rows - 1 else inv)
                coef[2, r, here, span] = west * (first_row if r == PAD_R else inv)
                coef[3, r, here, span] = north * (jnp.where(sub == 7, last_col, inv) if tile == last_tile else inv)
                coef[4, r, here, span] = south * (jnp.where(sub == 0, first_col, inv) if tile == first_tile else inv)
                coef[5, r, here, span] = up * (jnp.where(lane >= LANES - R, 0.0, inv) if half else inv)
                coef[6, r, here, span] = down * (inv if half else jnp.where(lane < R, 0.0, inv))

    expand(own_cells)
    pass_x(0)
    pass_y(0)
    arrive([moving_0[n] for n in straight])
    middle_cells = [cell for cell in all_cells if cell not in own_cells and first_tile <= cell[1] <= last_tile]
    expand(middle_cells)
    arrive([moving_0[n] for n in slanted])
    expand([cell for cell in all_cells if cell not in own_cells + middle_cells])
    pass_y(1)
    arrive(moving_1)
    pass_x(1)

    def apply(ref, r, cut):
        height = cols + 2 * PAD_C
        width = NZ * R
        centre = ref[r]
        north = pltpu.roll(centre, height - 1, 0)[cut]
        south = pltpu.roll(centre, 1, 0)[cut]
        middle = centre[cut]
        up = pltpu.roll(middle, width - R, 1)
        down = pltpu.roll(middle, R, 1)
        return (
            coef[0, r, cut, :] * middle
            - coef[1, r, cut, :] * ref[r + 1, cut, :]
            - coef[2, r, cut, :] * ref[r - 1, cut, :]
            - coef[3, r, cut, :] * north
            - coef[4, r, cut, :] * south
            - coef[5, r, cut, :] * up
            - coef[6, r, cut, :] * down
        )

    height = cols + 2 * PAD_C
    lanes = lax.broadcasted_iota(jnp.int32, (height, NZ * R), 1)
    place = lax.broadcasted_iota(jnp.int32, (height, NZ * R), 0) + (gy * cols - PAD_C)
    aim = jnp.full((height, NZ * R), -1 << 30, jnp.int32)
    for q in range(R):
        aim = jnp.where(lanes == R + q, aims[q], aim)
    aim = aim - place
    for r in range(PAD_R - FIRST + 1, PAD_R + rows + FIRST - 1):
        source = jnp.where(aim == (gx * rows + (r - PAD_R)) * (ny * cols), source_gain, 0.0)
        cut = slice(PAD_C, PAD_C + cols) if r in (PAD_R - FIRST + 1, PAD_R + rows + FIRST - 2) else slice(0, height)
        basis[0, r, cut, :] = source[cut] - (SCALE * apply(start, r, cut) + SHIFT * start[r, cut, :])

    def advance(j, reach):
        for r in range(PAD_R - reach, PAD_R + rows + reach):
            outer = reach == 0 or r in (PAD_R - reach, PAD_R + rows + reach - 1)
            cut = slice(PAD_C, PAD_C + cols) if outer else slice(0, height)
            basis[j, r, cut, :] = apply(basis.at[j - 1], r, cut)

    def products(a):
        spots = [
            (r, c, half)
            for r in range(PAD_R, PAD_R + rows)
            for c in range(PAD_C, PAD_C + cols, 8)
            for half in range(2)
        ]
        values = [basis[a, r, c : c + 8, half * LANES : (half + 1) * LANES] for r, c, half in spots]
        peaks[a] = tree([jnp.abs(value) for value in values], jnp.maximum)
        anchors = [(4.0 * len(spots)) * (peaks[a] * peaks[b]) for b in range(a + 1)]
        totals, errors = list(anchors), [None] * (a + 1)
        for n, value in enumerate(values):
            high, low = split(value)
            halves[a, n, 0], halves[a, n, 1] = high, low
            for b in range(a + 1):
                high_b, low_b = (high, low) if b == a else (halves[b, n, 0], halves[b, n, 1])
                exact = high * high_b
                small = high * low_b + low * (high_b + low_b)
                total = totals[b] + exact
                small = small + (exact - (total - totals[b]))
                totals[b], errors[b] = total, small if n == 0 else errors[b] + small
        for b in range(a + 1):
            sums[a, b] = (totals[b] - anchors[b], errors[b])

    def turn(value, shift, axis):
        return pltpu.roll(value, shift % value.shape[axis], axis)

    def weave(x, y, bit, axis):
        low = ((sub if axis == 0 else lane) & bit) == 0
        near = tuple(jnp.where(low, u, v) for u, v in zip(x, y))
        far = tuple(jnp.where(low, turn(u, -bit, axis), turn(v, bit, axis)) for u, v in zip(x, y))
        return pair_add(near, far)

    def stack(pairs):
        zero = jnp.zeros((8, LANES), jnp.float32)
        got = [sums[pair] if pair else (zero, zero) for pair in pairs]
        for bit in (4, 2, 1):
            got = [weave(got[n], got[n + bit], bit, 0) for n in range(bit)]
        return got[0]

    sums, peaks = {}, {}
    blocks = [PAIRS[n : n + 8] for n in range(0, len(PAIRS), 8)]
    blocks[-1] += [None] * (8 - len(blocks[-1]))
    for j in range(1, FIRST):
        advance(j, FIRST - 1 - j)
    moving_2 = exchange(basis.at[FIRST - 1], 2, DEGREE + 1 - FIRST)
    depart(moving_2)
    for a in range(FIRST):
        products(a)
    stacked = [stack(block) for block in blocks if block[-1] and block[-1][0] < FIRST]
    pass_y(2)
    arrive(moving_2)
    pass_x(2)
    pass_y(3)
    for j in range(FIRST, DEGREE + 1):
        advance(j, DEGREE - j)
        products(j)
    stacked += [stack(block) for block in blocks[len(stacked) :]]

    quarter = [weave(stacked[n], stacked[n + 2], 64, 1) for n in range(2)]
    folded = weave(quarter[0], quarter[1], 32, 1)
    folded = weave(folded, folded, 16, 1)
    folded = weave(folded, folded, 8, 1)
    chosen = (lane // R) % 4 == sub % 4
    for n, value in enumerate(folded):
        value = jnp.where(chosen, value, 0.0)
        mine[n, 0:1, :] = jnp.sum(value[0:4], axis=0, keepdims=True)
        mine[n, 1:2, :] = jnp.sum(value[4:8], axis=0, keepdims=True)

    def gather(src, dst, index, count, send_sem, recv_sem, to):
        copies = [
            pltpu.make_async_remote_copy(
                src_ref=src,
                dst_ref=dst.at[index],
                send_sem=send_sem,
                recv_sem=recv_sem,
                device_id=to(d),
                device_id_type=pl.DeviceIdType.MESH,
            )
            for d in sorted(range(1, count), key=lambda d: -min(d, count - d))
        ]
        for copy in copies:
            copy.start()
        dst[index] = src[...]
        some = dst.at[pl.ds(0, count - 1)]
        pltpu.make_async_copy(some, some, recv_sem).wait()
        total = tree([(dst[n, 0], dst[n, 1]) for n in range(count)], pair_add)
        return total, pltpu.make_async_copy(some, some, send_sem)

    for n in range(3, len(rounds_x)):
        pass_x(n)
    line_sum, line_left = gather(mine, line_in, gx, nx, line_send, line_recv, lambda d: peer(d, 0))
    line[0], line[1] = line_sum
    for n in range(4, len(rounds_y)):
        pass_y(n)
    total, plane_left = gather(line, plane_in, gy, ny, plane_send, plane_recv, lambda d: peer(0, d))

    value, error = total
    value, error = two_sum(value, error)
    upper = sub < 4
    for z in range(4):
        index = 32 * z + R * (sub % 4) + lane % R
        spread_out = lambda x: jnp.take_along_axis(
            jnp.where(upper, jnp.broadcast_to(x[0:1], (8, LANES)), jnp.broadcast_to(x[1:2], (8, LANES))), index, axis=1
        )
        here = spread_out(value)
        gram[0, 8 * z : 8 * z + 8, :] = here
        gram[1, 8 * z : 8 * z + 8, :] = spread_out(error)
        gram[2, 8 * z : 8 * z + 8, :], gram[3, 8 * z : 8 * z + 8, :] = split(here)

    def product(a, b):
        whole, high, low = b
        top = a[0] * whole
        return top, (((a[2] * high - top) + a[2] * low + a[3] * high) + a[3] * low) + a[1] * whole

    def entry(i, j):
        n = SLOT[max(i, j), min(i, j)]
        return tuple(gram[k, n : n + 1, :] for k in range(4))

    def with_halves(values):
        return [(value,) + split(value) for value in values]

    def pull(values, count):
        out = []
        for i in range(count):
            total, error = tree([product(entry(i, j), value) for j, value in enumerate(values)], pair_add)
            total, error = two_sum(total, error)
            out.append((total, error) + split(total))
        return out

    def inner(pulled, values):
        total, error = tree([product(a, b) for a, b in zip(pulled, values)], pair_add)
        return total + error

    shift = SHIFT / SCALE

    def operate(d):
        out = []
        for j in range(len(d) + 1):
            terms = ([shift * d[j]] if j < len(d) else []) + ([d[j - 1]] if j else [])
            out.append(terms[0] if len(terms) == 1 else terms[0] + terms[1])
        return out

    d = [jnp.ones((1, LANES), jnp.float32)]
    y = [jnp.zeros((1, LANES), jnp.float32) for _ in range(DEGREE)]
    for _ in range(CYCLES):
        image = operate(d)
        held, moved = with_halves(d), with_halves(image)
        pulled = pull(held, len(image))
        alpha = inner(pulled, held) / inner(pulled, moved)
        half_way = [(d[i] - alpha * image[i]) if i < len(d) else -(alpha * image[i]) for i in range(len(image))]
        turned = operate(half_way)
        held, moved = with_halves(half_way), with_halves(turned)
        pulled = pull(moved, len(turned))
        omega = inner(pulled, held) / inner(pulled, moved)
        for i in range(len(d)):
            y[i] = y[i] + alpha * d[i]
        for i in range(len(half_way)):
            y[i] = y[i] + omega * half_way[i]
        d = [
            (half_way[i] - omega * turned[i]) if i < len(half_way) else -(omega * turned[i])
            for i in range(len(turned))
        ]

    steps = [value * inv for value in y]
    for r in range(rows):
        for c in range(0, cols, 8):
            for half in range(2):
                span = slice(half * LANES, (half + 1) * LANES)
                held = [basis[j, PAD_R + r, PAD_C + c : PAD_C + c + 8, span] for j in range(DEGREE + 1)]
                moved = tree([steps[j] * held[j] for j in range(DEGREE)], jnp.add)
                out[0, r, c : c + 8, span] = start[PAD_R + r, PAD_C + c : PAD_C + c + 8, span] + moved
                out[1, r, c : c + 8, span] = tree([d[j] * held[j] for j in range(DEGREE + 1)], jnp.add)

    for dy, copy in moving_0 + moving_1 + moving_2:
        where_inside(dy, copy.wait_send)
    plane_left.wait()
    line_left.wait()


def solution(mesh):
    nx, ny = mesh.shape["gx"], mesh.shape["gy"]

    def body(*arrays):
        adjoint_guess, velocity, leaf_rate, canopy, solid, receptors = arrays
        rows, cols = adjoint_guess.shape[0], adjoint_guess.shape[1]
        tall, wide = rows + 2 * PAD_R, cols + 2 * PAD_C
        shape = jax.ShapeDtypeStruct((2,) + adjoint_guess.shape, jnp.float32)
        both = pl.pallas_call(
            functools.partial(kernel, nx, ny, rows, cols),
            out_shape=shape,
            in_specs=[pl.BlockSpec(memory_space=pltpu.HBM)] * 6,
            out_specs=pl.BlockSpec(memory_space=pltpu.VMEM),
            scratch_shapes=[
                pltpu.VMEM((tall, wide, NZ * R), jnp.float32),
                pltpu.VMEM((DEGREE + 1, tall, wide, NZ * R), jnp.float32),
                pltpu.VMEM((tall, wide, LANES), jnp.float32),
                pltpu.VMEM((7, tall, wide, NZ * R), jnp.float32),
                pltpu.VMEM(velocity.shape, jnp.float32),
                pltpu.VMEM(leaf_rate.shape, jnp.float32),
                pltpu.VMEM(canopy.shape, jnp.int32),
                pltpu.VMEM(solid.shape, jnp.int32),
                pltpu.VMEM((DEGREE + 1, rows * cols * 2 // 8, 2, 8, LANES), jnp.float32),
                pltpu.VMEM((4, 32, LANES), jnp.float32),
                pltpu.VMEM((2, 2, LANES), jnp.float32),
                pltpu.VMEM((ny, 2, 2, LANES), jnp.float32),
                pltpu.VMEM((2, 2, LANES), jnp.float32),
                pltpu.VMEM((nx, 2, 2, LANES), jnp.float32),
                pltpu.SMEM(receptors.shape, jnp.int32),
                pltpu.SemaphoreType.DMA((6,)),
                pltpu.SemaphoreType.DMA((3, len(SIDES))),
                pltpu.SemaphoreType.DMA((3, len(SIDES))),
                pltpu.SemaphoreType.DMA,
                pltpu.SemaphoreType.DMA,
                pltpu.SemaphoreType.DMA,
                pltpu.SemaphoreType.DMA,
                pltpu.SemaphoreType.REGULAR((8,)),
                pltpu.SemaphoreType.REGULAR((8,)),
            ],
            compiler_params=pltpu.CompilerParams(collective_id=0, has_side_effects=True, vmem_limit_bytes=16 << 20),
        )(*(pltpu.with_memory_space_constraint(array, pltpu.HBM) for array in arrays))
        return both[0], both[1]

    return jax.shard_map(
        body,
        mesh=mesh,
        in_specs=(
            P("gx", "gy", None),
            P(None, "gx", "gy"),
            P("gx", "gy"),
            P("gx", "gy"),
            P("gx", "gy"),
            P(),
        ),
        out_specs=(P("gx", "gy", None), P("gx", "gy", None)),
        check_vma=False,
    )
```

```python
import functools

import jax
import jax.numpy as jnp
from jax import lax
from jax.experimental import pallas as pl
from jax.experimental.pallas import tpu as pltpu
from jax.sharding import PartitionSpec as P

NZ = 32
R = 8
CYCLES = 3
DEGREE = 2 * CYCLES

horiz_diff = 4.0
vert_diff = 2.0
decay_rate = 3.5
penalty = 40.0
leaf_gain = 4.0
source_gain = 32.0

SHIFT = 27.0
SCALE = 16.0

FIRST = 4
PAD_R = 4
PAD_C = 8
LANES = 128

PAIRS = [(a, b) for a in range(DEGREE + 1) for b in range(a + 1)]
SLOT = {pair: n for n, pair in enumerate(PAIRS)}
SIDES = [(1, 1), (1, -1), (-1, 1), (-1, -1), (0, 1), (0, -1), (1, 0), (-1, 0)]


def window(delta, reach, own, pad):
    if delta == 0:
        return pl.ds(pad, own), pl.ds(pad, own)
    if delta > 0:
        return pl.ds(pad + own - reach, reach), pl.ds(pad - reach, reach)
    return pl.ds(pad, reach), pl.ds(pad + own, reach)


def two_sum(a, b):
    total = a + b
    back = total - a
    return total, (a - (total - back)) + (b - back)


def pair_add(a, b):
    total, error = two_sum(a[0], b[0])
    return total, error + (a[1] + b[1])


def split(value):
    scaled = value * 4097.0
    high = scaled - (scaled - value)
    return high, value - high


def tree(terms, join):
    terms = list(terms)
    while len(terms) > 1:
        terms = [join(terms[n], terms[n + 1]) if n + 1 < len(terms) else terms[n] for n in range(0, len(terms), 2)]
    return terms[0]


def kernel(
    nx, ny, rows, cols,
    guess, velocity, leaf, canopy, solid, receptors,
    out,
    start, basis, packed, coef, raw_vel, raw_leaf, raw_canopy, raw_solid,
    halves, gram, mine, plane_in, line, line_in, aims,
    load_sem, halo_send, halo_recv, plane_send, plane_recv, line_send, line_recv, met_x, met_y,
):
    gx = lax.axis_index("gx")
    gy = lax.axis_index("gy")

    def peer(dx, dy):
        return {
            "gx": lax.rem(gx + dx + nx, nx) if dx else gx,
            "gy": lax.rem(gy + dy + ny, ny) if dy else gy,
        }

    def inside(dy):
        return jnp.logical_and(gy + dy >= 0, gy + dy < ny)

    def where_inside(dy, act):
        if dy:
            pl.when(inside(dy))(act)
        else:
            act()

    def signal(sem, side):
        where_inside(
            side[1],
            lambda: pl.semaphore_signal(sem, inc=1, device_id=peer(*side), device_id_type=pl.DeviceIdType.MESH),
        )

    def both(d):
        return inside(d).astype(jnp.int32) + inside(-d).astype(jnp.int32)

    barrier = pltpu.get_barrier_semaphore()
    for side in SIDES:
        signal(barrier, side)

    def rounds(most):
        reach, out = 1, []
        while reach < most:
            out.append(reach)
            reach *= 2
        return out

    rounds_x, rounds_y = rounds(nx // 2), rounds(ny - 1)

    def tell_x(n):
        if n < len(rounds_x):
            for d in (rounds_x[n], -rounds_x[n]):
                signal(met_x.at[n], (d, 0))

    def tell_y(n):
        if n < len(rounds_y):
            for d in (rounds_y[n], -rounds_y[n]):
                signal(met_y.at[n], (0, d))

    def pass_x(n):
        if n < len(rounds_x):
            pl.semaphore_wait(met_x.at[n], 2)
            tell_x(n + 1)

    def pass_y(n):
        if n < len(rounds_y):
            pl.semaphore_wait(met_y.at[n], both(rounds_y[n]))
            tell_y(n + 1)


    own_r, own_c = pl.ds(PAD_R, rows), pl.ds(PAD_C, cols)
    loads = [
        pltpu.make_async_copy(velocity, raw_vel, load_sem.at[0]),
        pltpu.make_async_copy(leaf, raw_leaf, load_sem.at[1]),
        pltpu.make_async_copy(canopy, raw_canopy, load_sem.at[2]),
        pltpu.make_async_copy(solid, raw_solid, load_sem.at[3]),
        pltpu.make_async_copy(guess, start.at[own_r, own_c], load_sem.at[4]),
        pltpu.make_async_copy(receptors, aims, load_sem.at[5]),
    ]
    for copy in loads:
        copy.start()

    def clear(side):
        for ref in (start, packed, basis.at[FIRST - 1]):
            ref[:, side, :] = jnp.zeros((ref.shape[0], PAD_C, ref.shape[2]), jnp.float32)

    pl.when(gy == 0)(lambda: clear(slice(0, PAD_C)))
    pl.when(gy == ny - 1)(lambda: clear(slice(PAD_C + cols, 2 * PAD_C + cols)))

    sub = lax.broadcasted_iota(jnp.int32, (8, LANES), 0)
    lane = lax.broadcasted_iota(jnp.int32, (8, LANES), 1)

    for copy in loads[:4]:
        copy.wait()
    reaction = penalty * raw_solid[...].astype(jnp.float32) + leaf_gain * raw_leaf[...] * raw_canopy[...].astype(jnp.float32)
    parts = [raw_vel[0], raw_vel[1], raw_vel[2], reaction]
    spread = (sub % 4) * NZ + lane % NZ
    for i in range(rows):
        for tile in range(cols // 8):
            total = None
            for n, part in enumerate(parts):
                low = jnp.broadcast_to(part[i : i + 1, (2 * tile) * LANES : (2 * tile + 1) * LANES], (8, LANES))
                high = jnp.broadcast_to(part[i : i + 1, (2 * tile + 1) * LANES : (2 * tile + 2) * LANES], (8, LANES))
                value = jnp.take_along_axis(jnp.where(sub < 4, low, high), spread, axis=1)
                total = value if total is None else jnp.where(lane // NZ == n, value, total)
            packed[PAD_R + i, PAD_C + 8 * tile : PAD_C + 8 * tile + 8, :] = total

    for copy in loads[4:]:
        copy.wait()
    pl.semaphore_wait(barrier, 3 * (1 + both(1)) - 1)

    reach = max(FIRST - 1, DEGREE - FIRST)

    def exchange(ref, bank, reach):
        copies = []
        for n, (dx, dy) in enumerate(SIDES):
            near = reach - 1 if dx and dy else reach
            src_r, dst_r = window(dx, near, rows, PAD_R)
            src_c, dst_c = window(dy, near, cols, PAD_C)
            copies.append(
                (
                    dy,
                    pltpu.make_async_remote_copy(
                        src_ref=ref.at[src_r, src_c],
                        dst_ref=ref.at[dst_r, dst_c],
                        send_sem=halo_send.at[bank, n],
                        recv_sem=halo_recv.at[bank, n],
                        device_id=peer(dx, dy),
                        device_id_type=pl.DeviceIdType.MESH,
                    ),
                )
            )
        return copies

    def depart(copies):
        for dy, copy in copies:
            where_inside(dy, copy.start)

    def arrive(copies):
        for dy, copy in copies:
            where_inside(-dy, copy.wait_recv)

    straight = [n for n, (dx, dy) in enumerate(SIDES) if not dy]
    slanted = [n for n, (dx, dy) in enumerate(SIDES) if dy]

    moving_0 = exchange(packed, 0, reach)
    moving_1 = exchange(start, 1, FIRST)
    for group in (slanted, straight):
        depart([moving_0[n] for n in group])
        depart([moving_1[n] for n in group])
    tell_x(0)
    tell_y(0)

    inv = 1.0 / SCALE
    first_row = jnp.where(gx == 0, 0.0, inv)
    last_row = jnp.where(gx == nx - 1, 0.0, inv)
    first_col = jnp.where(gy == 0, 0.0, inv)
    last_col = jnp.where(gy == ny - 1, 0.0, inv)
    tiles = (cols + 2 * PAD_C) // 8
    first_tile, last_tile = PAD_C // 8, (PAD_C + cols) // 8 - 1
    own_cells = [(r, tile) for r in range(PAD_R, PAD_R + rows) for tile in range(first_tile, last_tile + 1)]
    all_cells = [
        (r, tile)
        for r in range(PAD_R - reach, PAD_R + rows + reach)
        for tile in range(tiles)
        if PAD_R - reach < r < PAD_R + rows + reach - 1 or first_tile <= tile <= last_tile
    ]

    def expand(cells):
        for r, tile in cells:
            here = pl.ds(8 * tile, 8)
            cell = packed[r, 8 * tile : 8 * tile + 8, :]
            for half in range(2):
                span = slice(half * LANES, (half + 1) * LANES)
                level = lane // R + half * (LANES // R)
                u, v, w, react = (jnp.take_along_axis(cell, n * NZ + level, axis=1) for n in range(4))
                relu = lambda value: jnp.maximum(value, 0.0)
                east, west = horiz_diff + relu(u), horiz_diff + relu(-u)
                north, south = horiz_diff + relu(v), horiz_diff + relu(-v)
                up, down = vert_diff + relu(w), vert_diff + relu(-w)
                diag = decay_rate + react + east + west + north + south + up + down
                coef[0, r, here, span] = (diag - SHIFT) * inv
                coef[1, r, here, span] = east * (last_row if r == PAD_R + rows - 1 else inv)
                coef[2, r, here, span] = west * (first_row if r == PAD_R else inv)
                coef[3, r, here, span] = north * (jnp.where(sub == 7, last_col, inv) if tile == last_tile else inv)
                coef[4, r, here, span] = south * (jnp.where(sub == 0, first_col, inv) if tile == first_tile else inv)
                coef[5, r, here, span] = up * (jnp.where(lane >= LANES - R, 0.0, inv) if half else inv)
                coef[6, r, here, span] = down * (inv if half else jnp.where(lane < R, 0.0, inv))

    expand(own_cells)
    pass_x(0)
    pass_y(0)
    arrive([moving_0[n] for n in straight])
    middle_cells = [cell for cell in all_cells if cell not in own_cells and first_tile <= cell[1] <= last_tile]
    expand(middle_cells)
    arrive([moving_0[n] for n in slanted])
    expand([cell for cell in all_cells if cell not in own_cells + middle_cells])
    arrive(moving_1)
    pass_x(1)

    def apply(ref, r, cut):
        height = cols + 2 * PAD_C
        width = NZ * R
        centre = ref[r]
        north = pltpu.roll(centre, height - 1, 0)[cut]
        south = pltpu.roll(centre, 1, 0)[cut]
        middle = centre[cut]
        up = pltpu.roll(middle, width - R, 1)
        down = pltpu.roll(middle, R, 1)
        return (
            coef[0, r, cut, :] * middle
            - coef[1, r, cut, :] * ref[r + 1, cut, :]
            - coef[2, r, cut, :] * ref[r - 1, cut, :]
            - coef[3, r, cut, :] * north
            - coef[4, r, cut, :] * south
            - coef[5, r, cut, :] * up
            - coef[6, r, cut, :] * down
        )

    height = cols + 2 * PAD_C
    lanes = lax.broadcasted_iota(jnp.int32, (height, NZ * R), 1)
    place = lax.broadcasted_iota(jnp.int32, (height, NZ * R), 0) + (gy * cols - PAD_C)
    aim = jnp.full((height, NZ * R), -1 << 30, jnp.int32)
    for q in range(R):
        aim = jnp.where(lanes == R + q, aims[q], aim)
    aim = aim - place
    for r in range(PAD_R - FIRST + 1, PAD_R + rows + FIRST - 1):
        source = jnp.where(aim == (gx * rows + (r - PAD_R)) * (ny * cols), source_gain, 0.0)
        cut = slice(PAD_C, PAD_C + cols) if r in (PAD_R - FIRST + 1, PAD_R + rows + FIRST - 2) else slice(0, height)
        basis[0, r, cut, :] = source[cut] - (SCALE * apply(start, r, cut) + SHIFT * start[r, cut, :])

    def advance(j, reach):
        for r in range(PAD_R - reach, PAD_R + rows + reach):
            outer = reach == 0 or r in (PAD_R - reach, PAD_R + rows + reach - 1)
            cut = slice(PAD_C, PAD_C + cols) if outer else slice(0, height)
            basis[j, r, cut, :] = apply(basis.at[j - 1], r, cut)

    def products(a):
        spots = [
            (r, c, half)
            for r in range(PAD_R, PAD_R + rows)
            for c in range(PAD_C, PAD_C + cols, 8)
            for half in range(2)
        ]
        values = [basis[a, r, c : c + 8, half * LANES : (half + 1) * LANES] for r, c, half in spots]
        peaks[a] = tree([jnp.abs(value) for value in values], jnp.maximum)
        anchors = [(4.0 * len(spots)) * (peaks[a] * peaks[b]) for b in range(a + 1)]
        totals, errors = list(anchors), [None] * (a + 1)
        for n, value in enumerate(values):
            high, low = split(value)
            halves[a, n, 0], halves[a, n, 1] = high, low
            for b in range(a + 1):
                high_b, low_b = (high, low) if b == a else (halves[b, n, 0], halves[b, n, 1])
                exact = high * high_b
                small = high * low_b + low * (high_b + low_b)
                total = totals[b] + exact
                small = small + (exact - (total - totals[b]))
                totals[b], errors[b] = total, small if n == 0 else errors[b] + small
        for b in range(a + 1):
            sums[a, b] = (totals[b] - anchors[b], errors[b])

    def turn(value, shift, axis):
        return pltpu.roll(value, shift % value.shape[axis], axis)

    def weave(x, y, bit, axis):
        low = ((sub if axis == 0 else lane) & bit) == 0
        near = tuple(jnp.where(low, u, v) for u, v in zip(x, y))
        far = tuple(jnp.where(low, turn(u, -bit, axis), turn(v, bit, axis)) for u, v in zip(x, y))
        return pair_add(near, far)

    def stack(pairs):
        zero = jnp.zeros((8, LANES), jnp.float32)
        got = [sums[pair] if pair else (zero, zero) for pair in pairs]
        for bit in (4, 2, 1):
            got = [weave(got[n], got[n + bit], bit, 0) for n in range(bit)]
        return got[0]

    sums, peaks = {}, {}
    blocks = [PAIRS[n : n + 8] for n in range(0, len(PAIRS), 8)]
    blocks[-1] += [None] * (8 - len(blocks[-1]))
    for j in range(1, FIRST):
        advance(j, FIRST - 1 - j)
    moving_2 = exchange(basis.at[FIRST - 1], 2, DEGREE + 1 - FIRST)
    depart(moving_2)
    pass_y(1)
    for a in range(FIRST):
        products(a)
    stacked = [stack(block) for block in blocks if block[-1] and block[-1][0] < FIRST]
    pass_y(2)
    arrive(moving_2)
    pass_x(2)
    pass_y(3)
    for j in range(FIRST, DEGREE + 1):
        advance(j, DEGREE - j)
        products(j)
    stacked += [stack(block) for block in blocks[len(stacked) :]]

    quarter = [weave(stacked[n], stacked[n + 2], 64, 1) for n in range(2)]
    folded = weave(quarter[0], quarter[1], 32, 1)
    folded = weave(folded, folded, 16, 1)
    folded = weave(folded, folded, 8, 1)
    chosen = (lane // R) % 4 == sub % 4
    for n, value in enumerate(folded):
        value = jnp.where(chosen, value, 0.0)
        mine[n, 0:1, :] = jnp.sum(value[0:4], axis=0, keepdims=True)
        mine[n, 1:2, :] = jnp.sum(value[4:8], axis=0, keepdims=True)

    def gather(src, dst, index, count, send_sem, recv_sem, to):
        copies = [
            pltpu.make_async_remote_copy(
                src_ref=src,
                dst_ref=dst.at[index],
                send_sem=send_sem,
                recv_sem=recv_sem,
                device_id=to(d),
                device_id_type=pl.DeviceIdType.MESH,
            )
            for d in sorted(range(1, count), key=lambda d: -min(d, count - d))
        ]
        for copy in copies:
            copy.start()
        dst[index] = src[...]
        some = dst.at[pl.ds(0, count - 1)]
        pltpu.make_async_copy(some, some, recv_sem).wait()
        total = tree([(dst[n, 0], dst[n, 1]) for n in range(count)], pair_add)
        return total, pltpu.make_async_copy(some, some, send_sem)

    for n in range(3, len(rounds_x)):
        pass_x(n)
    line_sum, line_left = gather(mine, line_in, gx, nx, line_send, line_recv, lambda d: peer(d, 0))
    line[0], line[1] = line_sum
    for n in range(4, len(rounds_y)):
        pass_y(n)
    total, plane_left = gather(line, plane_in, gy, ny, plane_send, plane_recv, lambda d: peer(0, d))

    value, error = total
    value, error = two_sum(value, error)
    upper = sub < 4
    for z in range(4):
        index = 32 * z + R * (sub % 4) + lane % R
        spread_out = lambda x: jnp.take_along_axis(
            jnp.where(upper, jnp.broadcast_to(x[0:1], (8, LANES)), jnp.broadcast_to(x[1:2], (8, LANES))), index, axis=1
        )
        here = spread_out(value)
        gram[0, 8 * z : 8 * z + 8, :] = here
        gram[1, 8 * z : 8 * z + 8, :] = spread_out(error)
        gram[2, 8 * z : 8 * z + 8, :], gram[3, 8 * z : 8 * z + 8, :] = split(here)

    def product(a, b):
        whole, high, low = b
        top = a[0] * whole
        return top, (((a[2] * high - top) + a[2] * low + a[3] * high) + a[3] * low) + a[1] * whole

    def entry(i, j):
        n = SLOT[max(i, j), min(i, j)]
        return tuple(gram[k, n : n + 1, :] for k in range(4))

    def with_halves(values):
        return [(value,) + split(value) for value in values]

    def pull(values, count):
        out = []
        for i in range(count):
            total, error = tree([product(entry(i, j), value) for j, value in enumerate(values)], pair_add)
            total, error = two_sum(total, error)
            out.append((total, error) + split(total))
        return out

    def inner(pulled, values):
        total, error = tree([product(a, b) for a, b in zip(pulled, values)], pair_add)
        return total + error

    shift = SHIFT / SCALE

    def operate(d):
        out = []
        for j in range(len(d) + 1):
            terms = ([shift * d[j]] if j < len(d) else []) + ([d[j - 1]] if j else [])
            out.append(terms[0] if len(terms) == 1 else terms[0] + terms[1])
        return out

    d = [jnp.ones((1, LANES), jnp.float32)]
    y = [jnp.zeros((1, LANES), jnp.float32) for _ in range(DEGREE)]
    for _ in range(CYCLES):
        image = operate(d)
        held, moved = with_halves(d), with_halves(image)
        pulled = pull(held, len(image))
        alpha = inner(pulled, held) / inner(pulled, moved)
        half_way = [(d[i] - alpha * image[i]) if i < len(d) else -(alpha * image[i]) for i in range(len(image))]
        turned = operate(half_way)
        held, moved = with_halves(half_way), with_halves(turned)
        pulled = pull(moved, len(turned))
        omega = inner(pulled, held) / inner(pulled, moved)
        for i in range(len(d)):
            y[i] = y[i] + alpha * d[i]
        for i in range(len(half_way)):
            y[i] = y[i] + omega * half_way[i]
        d = [
            (half_way[i] - omega * turned[i]) if i < len(half_way) else -(omega * turned[i])
            for i in range(len(turned))
        ]

    steps = [value * inv for value in y]
    for r in range(rows):
        for c in range(0, cols, 8):
            for half in range(2):
                span = slice(half * LANES, (half + 1) * LANES)
                held = [basis[j, PAD_R + r, PAD_C + c : PAD_C + c + 8, span] for j in range(DEGREE + 1)]
                moved = tree([steps[j] * held[j] for j in range(DEGREE)], jnp.add)
                out[0, r, c : c + 8, span] = start[PAD_R + r, PAD_C + c : PAD_C + c + 8, span] + moved
                out[1, r, c : c + 8, span] = tree([d[j] * held[j] for j in range(DEGREE + 1)], jnp.add)

    for dy, copy in moving_0 + moving_1 + moving_2:
        where_inside(dy, copy.wait_send)
    plane_left.wait()
    line_left.wait()


def solution(mesh):
    nx, ny = mesh.shape["gx"], mesh.shape["gy"]

    def body(*arrays):
        adjoint_guess, velocity, leaf_rate, canopy, solid, receptors = arrays
        rows, cols = adjoint_guess.shape[0], adjoint_guess.shape[1]
        tall, wide = rows + 2 * PAD_R, cols + 2 * PAD_C
        shape = jax.ShapeDtypeStruct((2,) + adjoint_guess.shape, jnp.float32)
        both = pl.pallas_call(
            functools.partial(kernel, nx, ny, rows, cols),
            out_shape=shape,
            in_specs=[pl.BlockSpec(memory_space=pltpu.HBM)] * 6,
            out_specs=pl.BlockSpec(memory_space=pltpu.VMEM),
            scratch_shapes=[
                pltpu.VMEM((tall, wide, NZ * R), jnp.float32),
                pltpu.VMEM((DEGREE + 1, tall, wide, NZ * R), jnp.float32),
                pltpu.VMEM((tall, wide, LANES), jnp.float32),
                pltpu.VMEM((7, tall, wide, NZ * R), jnp.float32),
                pltpu.VMEM(velocity.shape, jnp.float32),
                pltpu.VMEM(leaf_rate.shape, jnp.float32),
                pltpu.VMEM(canopy.shape, jnp.int32),
                pltpu.VMEM(solid.shape, jnp.int32),
                pltpu.VMEM((DEGREE + 1, rows * cols * 2 // 8, 2, 8, LANES), jnp.float32),
                pltpu.VMEM((4, 32, LANES), jnp.float32),
                pltpu.VMEM((2, 2, LANES), jnp.float32),
                pltpu.VMEM((ny, 2, 2, LANES), jnp.float32),
                pltpu.VMEM((2, 2, LANES), jnp.float32),
                pltpu.VMEM((nx, 2, 2, LANES), jnp.float32),
                pltpu.SMEM(receptors.shape, jnp.int32),
                pltpu.SemaphoreType.DMA((6,)),
                pltpu.SemaphoreType.DMA((3, len(SIDES))),
                pltpu.SemaphoreType.DMA((3, len(SIDES))),
                pltpu.SemaphoreType.DMA,
                pltpu.SemaphoreType.DMA,
                pltpu.SemaphoreType.DMA,
                pltpu.SemaphoreType.DMA,
                pltpu.SemaphoreType.REGULAR((8,)),
                pltpu.SemaphoreType.REGULAR((8,)),
            ],
            compiler_params=pltpu.CompilerParams(collective_id=0, has_side_effects=True, vmem_limit_bytes=16 << 20),
        )(*(pltpu.with_memory_space_constraint(array, pltpu.HBM) for array in arrays))
        return both[0], both[1]

    return jax.shard_map(
        body,
        mesh=mesh,
        in_specs=(
            P("gx", "gy", None),
            P(None, "gx", "gy"),
            P("gx", "gy"),
            P("gx", "gy"),
            P("gx", "gy"),
            P(),
        ),
        out_specs=(P("gx", "gy", None), P("gx", "gy", None)),
        check_vma=False,
    )
```
